512 devices in a mesh: blk: 128 (over x, z_lo, y), rep: 4 (over z_hi, core).
Axes of the slice: x: 4, y: 4, z: 16 (z_hi: 2, z_lo: 8; z = z_hi * 8 + z_lo), core: 2. Of those that a mesh axis runs over, the one named last changes fastest.
Arguments:
- queries: bfloat16 [16384, 512], P('blk'), may hold values from -3.59375 to 3.59375
- keys: bfloat16 [16384, 128], P('blk'), may hold values from -6 to 6
- values: bfloat16 [16384, 128], P('blk'), may hold values from -6 to 6
- output: bfloat16 [16384, 512], P('blk'), may hold values from -6 to 6
- grad_out: bfloat16 [16384, 512], P('blk'), may hold values from -6 to 6
- lse: float32 [4, 16384], P(None, 'blk'), may hold values from -1 to 12.5
- positions: int32 [16384], P('blk'), may hold values from 0 to 1073741823, as said below
Outputs:
- grad_queries: bfloat16 [16384, 512], P('blk')
- grad_keys: bfloat16 [16384, 128], P('blk')
- grad_values: bfloat16 [16384, 128], P('blk')
The draws below stay inside these ranges and needn't reach their ends.
Inputs may be any that keep to these rules, and one draw needn't show every extreme that they name: positions are distinct. A token's place is the number of tokens with a smaller key. Cut the places into 2 n blocks of 64 consecutive places, n = 128; the rows of each index of blk hold the places of block c in order and then those of block 2 n - 1 - c in order, with c drawn at random for each index, every c once.
All inputs are finite; a program needn't handle non-finite values.
Results may differ from the reference program's by a relative error of at most 0.005.
Values may be sent and summed in bfloat16 or wider, within the bound.
A program may use at most 64 MiB of HBM per device.

```python
import jax
import jax.numpy as jnp
from jax import lax

HD = 128
HQ = 4
TOK_DEV = 128
TOKENS = 16384


def paired_rows(key):
    block_count = TOKENS // TOK_DEV
    half_rows = TOK_DEV // 2
    pairing = jax.random.permutation(jax.random.fold_in(key, 11), block_count).astype(jnp.int32)
    offsets = jnp.arange(half_rows, dtype=jnp.int32)
    lower = pairing[:, None] * half_rows + offsets[None, :]
    upper = (2 * block_count - 1 - pairing)[:, None] * half_rows + offsets[None, :]
    return jnp.concatenate([lower, upper], axis=1).reshape(TOKENS).astype(jnp.int32)


def draw_positions(key, part):
    places = paired_rows(key)
    stride = 2 ** 30 // TOKENS
    jitter = jax.random.randint(jax.random.fold_in(key, 37), (TOKENS,), 0, stride, dtype=jnp.int32)
    jitter = jnp.where(places == 0, 0, jitter)
    jitter = jnp.where(places == TOKENS - 1, stride - 1, jitter)
    return (places * stride + jitter).astype(jnp.int32)


def draw_lse(key, part):
    position = paired_rows(key).astype(jnp.float32)
    noise_key = jax.random.fold_in(key, 23)
    noise = jax.random.uniform(noise_key, (HQ, TOKENS), jnp.float32, -0.2, 0.2)
    return (jnp.log(position + 1.0) + 0.18)[None, :] + noise


def steps_of(own_key, shape, shards, least, top_value):
    level = 1.0
    for axis_at, shards_of in shards:
        draws = jax.random.uniform(jax.random.fold_in(jax.random.fold_in(own_key, 6), axis_at), (shards_of,), jnp.float32, least / len(shards), top_value / len(shards))
        level = level * jnp.repeat(jnp.exp(draws), shape[axis_at] // shards_of).reshape((-1,) + (1,) * (len(shape) - 1 - axis_at))
    return level


def bell_draw(rng, extent, spread, bound, shards=(), held_as=jnp.bfloat16):
    level = steps_of(rng, extent, shards, -0.22, 0.18) if shards else 1.0
    drawn = jax.random.normal(rng, extent, jnp.float32) * spread * level
    return jnp.minimum(jnp.maximum(drawn, -bound), bound).astype(held_as)


def setup_inputs(seed: int = 0) -> dict:
    seeds = jax.random.split(jax.random.key(seed), 8)
    queries = bell_draw(seeds[0], (TOKENS, HQ * HD), 0.6, 3.59375, ((0, 128),))
    keys = bell_draw(seeds[1], (TOKENS, HD), 1.0, 6.0, ((0, 128),))
    values = bell_draw(seeds[2], (TOKENS, HD), 1.0, 6.0, ((0, 128),))
    output = bell_draw(seeds[3], (TOKENS, HQ * HD), 1.0, 6.0, ((0, 128),))
    grad_out = bell_draw(seeds[4], (TOKENS, HQ * HD), 1.0, 6.0, ((0, 128),))
    lse = draw_lse(jax.random.fold_in(seeds[7], 71), 0)
    positions = draw_positions(jax.random.fold_in(seeds[7], 71), 0)
    return dict(queries=queries, keys=keys, values=values, output=output, grad_out=grad_out, lse=lse, positions=positions)


def reference(queries, keys, values, output, grad_out, lse, positions):
    sort_order = jnp.argsort(positions).astype(jnp.int32)
    place_of = jnp.argsort(sort_order).astype(jnp.int32)
    total_rows = positions.shape[0]
    head_dim = keys.shape[1]
    head_count = queries.shape[1] // head_dim
    score_scale = head_dim ** -0.5
    query_sorted = queries[sort_order].reshape(total_rows, head_count, head_dim).astype(jnp.float32)
    grad_sorted = grad_out[sort_order].reshape(total_rows, head_count, head_dim).astype(jnp.float32)
    out_sorted = output[sort_order].reshape(total_rows, head_count, head_dim).astype(jnp.float32)
    keys_sorted = keys[sort_order].astype(jnp.float32)
    values_sorted = values[sort_order].astype(jnp.float32)
    lse_sorted = lse[:, sort_order]
    row_delta = jnp.sum(grad_sorted * out_sorted, axis=2).T
    block_rows = 512 if total_rows % 512 == 0 else total_rows
    grad_keys = jnp.zeros((total_rows, head_dim), jnp.float32)
    grad_values = jnp.zeros((total_rows, head_dim), jnp.float32)
    query_parts = []
    for block in range(total_rows // block_rows):
        first = block * block_rows
        key_end = first + block_rows
        query_block = query_sorted[first:key_end]
        grad_block = grad_sorted[first:key_end]
        key_block = keys_sorted[:key_end]
        value_block = values_sorted[:key_end]
        row_index = jnp.arange(first, key_end)
        col_index = jnp.arange(key_end)
        visible = col_index[None, None, :] <= row_index[None, :, None]
        scores = jnp.einsum("thd,kd->htk", query_block, key_block) * score_scale
        probs = jnp.where(visible, jnp.exp(scores - lse_sorted[:, first:key_end, None]), 0.0)
        probs_low = lax.optimization_barrier(probs.astype(jnp.bfloat16)).astype(jnp.float32)
        grad_values = grad_values.at[:key_end].add(jnp.einsum("htk,thd->kd", probs_low, grad_block))
        grad_probs = jnp.einsum("thd,kd->htk", grad_block, value_block)
        grad_scores = probs * (grad_probs - row_delta[:, first:key_end, None]) * score_scale
        scores_low = lax.optimization_barrier(grad_scores.astype(jnp.bfloat16)).astype(jnp.float32)
        query_parts.append(jnp.einsum("htk,kd->thd", scores_low, key_block).reshape(block_rows, head_count * head_dim))
        grad_keys = grad_keys.at[:key_end].add(jnp.einsum("htk,thd->kd", scores_low, query_block))
    grad_query = jnp.concatenate(query_parts, axis=0)
    return (grad_query[place_of].astype(jnp.bfloat16), grad_keys[place_of].astype(jnp.bfloat16), grad_values[place_of].astype(jnp.bfloat16))
```

```python
import math

import jax
import jax.numpy as jnp
from jax import lax
from jax.experimental import pallas as pl
from jax.experimental.pallas import tpu as pltpu
from jax.sharding import PartitionSpec as P

MESH = pl.DeviceIdType.MESH
BF = jnp.bfloat16
F32 = jnp.float32
HD = 128
SCALE = HD ** (-0.5)
LOG2E = math.log2(math.e)
BIG = 1e30
NEAR = (0, 1, 7, 2, 6, 3, 5, 4)
FAR = (4, 3, 5, 2, 6, 1, 7, 0)


def coords():
    b = lax.axis_index("blk")
    r = lax.axis_index("rep")
    x = b // 32
    y = b % 4
    z = (r // 2) * 8 + (b // 4) % 8
    return x, y, z, r % 2


def dev(x, y, z, c):
    xx = (x + 4) % 4
    yy = (y + 4) % 4
    zz = (z + 16) % 16
    return ((xx * 8 + zz % 8) * 4 + yy, (zz // 8) * 2 + c)


def zoff(s, c):
    if s < 4:
        return s
    if s > 4:
        return s - 8
    return 4 - 8 * c


def peers(x, y, z, c):
    out = [dev(x, y, z, 1 - c)]
    for d in (1, 2, 3):
        out.append(dev(x + d, y, z, c))
        out.append(dev(x, y + d, z, c))
    for o in (1, 2, 3, 4, -1, -2, -3, -4):
        out.append(dev(x, y, z + o, c))
    return out


def entry_barrier(x, y, z, c):
    barrier = pltpu.get_barrier_semaphore()
    group = peers(x, y, z, c)
    for d in group:
        pl.semaphore_signal(barrier, inc=1, device_id=d, device_id_type=MESH)
    pl.semaphore_wait(barrier, len(group))


def rcopy(src, dst, ssem, rsem, device):
    return pltpu.make_async_remote_copy(
        src_ref=src, dst_ref=dst, send_sem=ssem, recv_sem=rsem, device_id=device, device_id_type=MESH
    )


def gather_kernel(
    q_ref, k_ref, v_ref, o_ref, do_ref, lse_ref, pos_ref,
    qd_ref, sm_ref, kv_ref, kp_ref,
    zs, zr, ps, pr, ys, yr, bs, br, xs, xr, ms, mr, kys, kyr,
):
    x, y, z, c = coords()
    col = pl.multiple_of(c * 256, 256)
    qd_ref[0, 0] = q_ref[:, pl.ds(col, 256)]
    qd_ref[0, 1] = do_ref[:, pl.ds(col, 256)]
    kv_ref[0, 0, 0] = k_ref[...]
    kv_ref[1, 0, 0] = v_ref[...]
    kp_ref[0, 0] = pos_ref[...]
    entry_barrier(x, y, z, c)

    started = []

    def go(cp):
        cp.start()
        started.append(cp)
        return cp

    zc = {}
    for s in NEAR[1:]:
        o = zoff(s, c)
        zc[s] = go(rcopy(kv_ref.at[c, 0, 0], kv_ref.at[c, s, 0], zs.at[s], zr.at[s], dev(x, y, z - o, c)))
    pc = {}
    for s in NEAR[1:]:
        o = zoff(s, c)
        pc[s] = go(rcopy(kp_ref.at[0, 0], kp_ref.at[0, s], ps.at[s], pr.at[s], dev(x, y, z - o, c)))
    xc = {
        3: go(rcopy(qd_ref.at[0], qd_ref.at[3], xs.at[3], xr.at[3], dev(x + 1, y, z, c))),
        1: go(rcopy(qd_ref.at[0], qd_ref.at[1], xs.at[1], xr.at[1], dev(x - 1, y, z, c))),
    }
    rows = []
    for h in range(2):
        rows.append(lse_ref[pl.ds(2 * c + h, 1), :])
    for h in range(2):
        prod = do_ref[:, pl.ds(col + h * HD, HD)].astype(F32) * o_ref[:, pl.ds(col + h * HD, HD)].astype(F32)
        tot = jnp.sum(prod, axis=1, keepdims=True)
        rows.append(jnp.broadcast_to(tot, (HD, HD)).T[0:1, :])
    p = pos_ref[...]
    rows.append((p // 32768).astype(F32))
    rows.append((p % 32768).astype(F32))
    rows.append(jnp.zeros((2, HD), F32))
    sm_ref[0] = jnp.concatenate(rows, axis=0)
    mc = {}
    for d in (1, 2, 3):
        mc[d] = go(rcopy(sm_ref.at[0], sm_ref.at[d], ms.at[d], mr.at[d], dev(x - d, y, z, c)))

    yc, hc, bc = {}, {}, {}

    def stage_full(s):
        if s:
            zc[s].wait_recv()
            bc[s, 0] = go(
                rcopy(kv_ref.at[c, s, 0], kv_ref.at[c, s, 0], bs.at[s, 0], br.at[s, 0], dev(x, y, z, 1 - c))
            )
        yc[s, 3] = go(rcopy(kv_ref.at[c, s, 0], kv_ref.at[c, s, 3], ys.at[s, 0], yr.at[s, 0], dev(x, y + 1, z, c)))
        yc[s, 1] = go(rcopy(kv_ref.at[c, s, 0], kv_ref.at[c, s, 1], ys.at[s, 1], yr.at[s, 1], dev(x, y - 1, z, c)))

    def stage_half(s):
        top, bot = pl.ds(0, 64), pl.ds(64, 64)
        yc[s, 3].wait_recv()
        hc[s, 0] = go(
            rcopy(kv_ref.at[c, s, 3, top], kv_ref.at[c, s, 2, top], ys.at[s, 2], yr.at[s, 2], dev(x, y + 1, z, c))
        )
        yc[s, 1].wait_recv()
        hc[s, 1] = go(
            rcopy(kv_ref.at[c, s, 1, bot], kv_ref.at[c, s, 2, bot], ys.at[s, 3], yr.at[s, 3], dev(x, y - 1, z, c))
        )

    def stage_sib(s):
        hc[s, 0].wait_recv()
        hc[s, 1].wait_recv()
        rest = pl.ds(1, 3)
        bc[s, 1] = go(
            rcopy(kv_ref.at[c, s, rest], kv_ref.at[c, s, rest], bs.at[s, 1], br.at[s, 1], dev(x, y, z, 1 - c))
        )

    xh = {}
    for t in range(len(NEAR) + 2):
        if t < 8:
            stage_full(NEAR[t])
        if t == 2:
            top, bot = pl.ds(0, 64), pl.ds(64, 64)
            both = pl.ds(0, 2)
            xc[3].wait_recv()
            xh[0] = go(
                rcopy(qd_ref.at[3, both, top], qd_ref.at[2, both, top], xs.at[0], xr.at[0], dev(x + 1, y, z, c))
            )
            xc[1].wait_recv()
            xh[1] = go(
                rcopy(qd_ref.at[1, both, bot], qd_ref.at[2, both, bot], xs.at[2], xr.at[2], dev(x - 1, y, z, c))
            )
        if 1 <= t < 9:
            stage_half(NEAR[t - 1])
        if 2 <= t:
            stage_sib(NEAR[t - 2])
    for s in NEAR[1:]:
        pc[s].wait_recv()
    kc = {}
    for d in (1, 2, 3):
        kc[d] = go(rcopy(kp_ref.at[0], kp_ref.at[d], kys.at[d], kyr.at[d], dev(x, y - d, z, c)))
    xh[0].wait_recv()
    xh[1].wait_recv()
    for d in (1, 2, 3):
        mc[d].wait_recv()
        kc[d].wait_recv()
    for s in range(8):
        if s:
            rcopy(
                kv_ref.at[1 - c, s, 0], kv_ref.at[1 - c, s, 0], bs.at[s, 0], br.at[s, 0], dev(x, y, z, 1 - c)
            ).wait_recv()
        rest = pl.ds(1, 3)
        rcopy(
            kv_ref.at[1 - c, s, rest], kv_ref.at[1 - c, s, rest], bs.at[s, 1], br.at[s, 1], dev(x, y, z, 1 - c)
        ).wait_recv()
    for cp in started:
        cp.wait_send()


def nt(a, b):
    return lax.dot_general(a, b, (((1,), (1,)), ((), ())), preferred_element_type=F32)


def nn(a, b):
    return lax.dot_general(a, b, (((1,), (0,)), ((), ())), preferred_element_type=F32)


def compute_kernel(qd_ref, sm_ref, kv_ref, kp_ref, dkv_ref, dq_ref, qx, dx, rw, dqt):
    lane = lax.broadcasted_iota(jnp.int32, (8, HD), 1)
    for i in range(4):
        for h in range(2):
            for half in range(2):
                rows = pl.ds(64 * half, 64)
                cols = pl.ds(HD * h, HD)
                qx[half, pl.ds(i * HD + 64 * h, 64), :] = qd_ref[i, 0, rows, cols]
                dx[half, pl.ds(i * HD + 64 * h, 64), :] = qd_ref[i, 1, rows, cols]
        t = sm_ref[i]
        tr = pltpu.roll(t, 64, 1)
        sel = lane < 64
        qlo = t[4:5].astype(jnp.int32) * 32768 + t[5:6].astype(jnp.int32)
        qlo = jnp.broadcast_to(qlo[:, 0:1], (1, HD)).astype(jnp.int32)
        cs = pl.ds(i * HD, HD)
        lse = t[0:2] * LOG2E
        lser = tr[0:2] * LOG2E
        rw[0:1, cs] = jnp.where(sel[0:1], lse[0:1], lser[1:2])
        rw[1:2, cs] = jnp.where(sel[0:1], lser[0:1], lse[1:2])
        rw[2:3, cs] = jnp.where(sel[0:1], t[2:3], tr[3:4]) * SCALE
        rw[3:4, cs] = jnp.where(sel[0:1], tr[2:3], t[3:4]) * SCALE
        rw[4:5, cs] = jnp.where(qlo < 0, 0, qlo // 32768).astype(F32)
        rw[5:6, cs] = (qlo % 32768).astype(F32)
    dqt[...] = jnp.zeros_like(dqt)

    def chunk(s, diag):
        firsts = []
        for yb in range(4):
            firsts.append(kp_ref[yb, s][:, 0:1])
        for kh in range(2):
            rows = pl.ds(64 * kh, 64)
            kc = kv_ref[0, s, :, rows, :].reshape(256, HD)
            vc = kv_ref[1, s, :, rows, :].reshape(256, HD)
            kt = kc.T
            dk = jnp.zeros((256, HD), F32)
            dv = jnp.zeros((256, HD), F32)
            for half in ((0, 1) if kh == 0 else (1,)):
                for g in range(2):
                    ls = pl.ds(256 * g, 256)
                    lse = rw[half : half + 1, ls]
                    dlt = rw[2 + half : 3 + half, ls]
                    if kh != half:
                        le = jnp.broadcast_to(lse, (4, 256))
                    else:
                        qp = rw[4:5, ls].astype(jnp.int32) * 32768 + rw[5:6, ls].astype(jnp.int32)
                        parts = []
                        for yb in range(4):
                            kp = jnp.broadcast_to(firsts[yb], (1, 256))
                            seen = kp <= qp if kh == 0 else kp >= qp
                            parts.append(jnp.where(seen, lse, BIG))
                        le = jnp.concatenate(parts, axis=0)
                    qg = qx[half, ls, :]
                    dg = dx[half, ls, :]
                    sc = nt(kc, qg).reshape(4, 64, 256)
                    dp = nt(vc, dg)
                    t = sc * (SCALE * LOG2E) - le[:, None, :]
                    t = t.reshape(256, 256)
                    if diag and kh == half and g == 0:
                        ri = lax.broadcasted_iota(jnp.int32, (256, 256), 0)
                        li = lax.broadcasted_iota(jnp.int32, (256, 256), 1)
                        seen = (ri >= 64) | (li >= 128) | (ri <= li % 64)
                        t = jnp.where(seen, t, -BIG)
                    p = jnp.exp2(t)
                    ds = (p * (dp * SCALE - dlt)).astype(BF)
                    dv = dv + nn(p.astype(BF), dg)
                    dk = dk + nn(ds, qg)
                    dqt[half, :, ls] += nn(kt, ds)
            dkv_ref[0, s, :, rows, :] = dk.astype(BF).reshape(4, 64, HD)
            dkv_ref[1, s, :, rows, :] = dv.astype(BF).reshape(4, 64, HD)

    chunk(0, True)

    def body(s, carry):
        chunk(s, False)
        return carry

    lax.fori_loop(1, 8, body, 0)
    for i in range(4):
        for half in range(2):
            tile = dqt[half, :, pl.ds(i * HD, HD)].T.astype(BF)
            for h in range(2):
                dq_ref[i, pl.ds(64 * half, 64), pl.ds(HD * h, HD)] = tile[64 * h : 64 * h + 64]


def reduce_kernel(
    dkv_ref, dq_ref,
    gq_ref, gk_ref, gv_ref,
    sib, acc, fa, fb, ra, rb, zb, zin, fin, qin, qfin,
    bs, br, ys, yr, zs, zr, xs, xr, fs, fr,
):
    x, y, z, c = coords()
    entry_barrier(x, y, z, c)
    started = []

    def go(cp):
        cp.start()
        started.append(cp)
        return cp

    other = dev(x, y, z, 1 - c)
    top, bot = pl.ds(0, 64), pl.ds(64, 64)
    bc, qc, ac, rc, zc = {}, {}, {}, {}, {}
    for s in FAR:
        bc[s] = go(rcopy(dkv_ref.at[1 - c, s], sib.at[s], bs.at[s], br.at[s], other))
    for d in (2, 1, 3):
        qc[d] = go(rcopy(dq_ref.at[d], qin.at[d], xs.at[d], xr.at[d], dev(x + d, y, z, c)))

    def stage_a(s):
        bc[s].wait_recv()
        for d in (2, 1, 3):
            acc[s, d] = (dkv_ref[c, s, d].astype(F32) + sib[s, d].astype(F32)).astype(BF)
        ac[s, 0] = go(rcopy(acc.at[s, 2, top], fa.at[s], ys.at[s, 0], yr.at[s, 0], dev(x, y + 1, z, c)))
        ac[s, 1] = go(rcopy(acc.at[s, 2, bot], fb.at[s], ys.at[s, 1], yr.at[s, 1], dev(x, y - 1, z, c)))

    def stage_b(s):
        ac[s, 0].wait_recv()
        acc[s, 1, top] = (acc[s, 1, top].astype(F32) + fa[s].astype(F32)).astype(BF)
        rc[s, 0] = go(rcopy(acc.at[s, 1], ra.at[s], ys.at[s, 2], yr.at[s, 2], dev(x, y + 1, z, c)))
        ac[s, 1].wait_recv()
        acc[s, 3, bot] = (acc[s, 3, bot].astype(F32) + fb[s].astype(F32)).astype(BF)
        rc[s, 1] = go(rcopy(acc.at[s, 3], rb.at[s], ys.at[s, 3], yr.at[s, 3], dev(x, y - 1, z, c)))

    def stage_c(s):
        rc[s, 0].wait_recv()
        rc[s, 1].wait_recv()
        tot = dkv_ref[c, s, 0].astype(F32) + sib[s, 0].astype(F32) + ra[s].astype(F32) + rb[s].astype(F32)
        if s == 0:
            return tot
        zb[s] = tot.astype(BF)
        o = zoff(s, c)
        zc[s] = go(rcopy(zb.at[s], zin.at[s], zs.at[s], zr.at[s], dev(x, y, z + o, c)))
        return None

    tot = None
    for t in range(10):
        if t < 8:
            stage_a(FAR[t])
        if 1 <= t < 9:
            stage_b(FAR[t - 1])
        if 2 <= t:
            tot = stage_c(FAR[t - 2])
    for d in (1, 2, 3):
        qc[d].wait_recv()
    qsum = dq_ref[0].astype(F32)
    for d in (1, 2, 3):
        qsum = qsum + qin[d].astype(F32)
    qfin[0] = qsum.astype(BF)
    sq = go(rcopy(qfin.at[0], qfin.at[1], fs.at[0], fr.at[0], other))
    for s in range(1, 8):
        zc[s].wait_recv()
        tot = tot + zin[s].astype(F32)
    fin[0] = tot.astype(BF)
    sk = go(rcopy(fin.at[0], fin.at[1], fs.at[1], fr.at[1], other))
    low = c == 0
    sq.wait_recv()
    gq_ref[:, 0:256] = jnp.where(low, qfin[0], qfin[1])
    gq_ref[:, 256:512] = jnp.where(low, qfin[1], qfin[0])
    sk.wait_recv()
    gk_ref[...] = jnp.where(low, fin[0], fin[1])
    gv_ref[...] = jnp.where(low, fin[1], fin[0])
    for cp in started:
        cp.wait_send()


VM = pl.BlockSpec(memory_space=pltpu.VMEM)
DMA = pltpu.SemaphoreType.DMA


def per_device(queries, keys, values, output, grad_out, lse, positions):
    shapes = (
        jax.ShapeDtypeStruct((4, 2, 128, 256), BF),
        jax.ShapeDtypeStruct((4, 8, 128), F32),
        jax.ShapeDtypeStruct((2, 8, 4, 128, 128), BF),
        jax.ShapeDtypeStruct((4, 8, 1, 128), jnp.int32),
    )
    qd, sm, kv, kp = pl.pallas_call(
        gather_kernel,
        out_shape=shapes,
        in_specs=[VM] * 7,
        out_specs=(VM,) * 4,
        scratch_shapes=[
            DMA((8,)), DMA((8,)), DMA((8,)), DMA((8,)), DMA((8, 4)), DMA((8, 4)), DMA((8, 2)), DMA((8, 2)),
            DMA((4,)), DMA((4,)), DMA((4,)), DMA((4,)), DMA((4,)), DMA((4,)),
        ],
        compiler_params=pltpu.CompilerParams(collective_id=0, has_side_effects=True),
        name="gather",
    )(queries, keys, values, output, grad_out, lse, positions.reshape(1, 128))
    dkv, dq = pl.pallas_call(
        compute_kernel,
        out_shape=(
            jax.ShapeDtypeStruct((2, 8, 4, 128, 128), BF),
            jax.ShapeDtypeStruct((4, 128, 256), BF),
        ),
        in_specs=[VM] * 4,
        out_specs=(VM,) * 2,
        scratch_shapes=[
            pltpu.VMEM((2, 512, 128), BF),
            pltpu.VMEM((2, 512, 128), BF),
            pltpu.VMEM((8, 512), F32),
            pltpu.VMEM((2, 128, 512), F32),
        ],
        name="compute",
    )(qd, sm, kv, kp)
    return pl.pallas_call(
        reduce_kernel,
        out_shape=(
            jax.ShapeDtypeStruct((128, 512), BF),
            jax.ShapeDtypeStruct((128, 128), BF),
            jax.ShapeDtypeStruct((128, 128), BF),
        ),
        in_specs=[VM] * 2,
        out_specs=(VM,) * 3,
        scratch_shapes=[
            pltpu.VMEM((8, 4, 128, 128), BF),
            pltpu.VMEM((8, 4, 128, 128), BF),
            pltpu.VMEM((8, 64, 128), BF),
            pltpu.VMEM((8, 64, 128), BF),
            pltpu.VMEM((8, 128, 128), BF),
            pltpu.VMEM((8, 128, 128), BF),
            pltpu.VMEM((8, 128, 128), BF),
            pltpu.VMEM((8, 128, 128), BF),
            pltpu.VMEM((2, 128, 128), BF),
            pltpu.VMEM((4, 128, 256), BF),
            pltpu.VMEM((2, 128, 256), BF),
            DMA((8,)), DMA((8,)), DMA((8, 4)), DMA((8, 4)), DMA((8,)), DMA((8,)), DMA((4,)), DMA((4,)),
            DMA((2,)), DMA((2,)),
        ],
        compiler_params=pltpu.CompilerParams(collective_id=1, has_side_effects=True),
        name="reduce",
    )(dkv, dq)


def solution(mesh):
    placed = (
        P("blk", None),
        P("blk", None),
        P("blk", None),
        P("blk", None),
        P("blk", None),
        P(None, "blk"),
        P("blk"),
    )
    return jax.shard_map(
        per_device,
        mesh=mesh,
        in_specs=placed,
        out_specs=(P("blk", None), P("blk", None), P("blk", None)),
        check_vma=False,
    )
```

```python
import math

import jax
import jax.numpy as jnp
from jax import lax
from jax.experimental import pallas as pl
from jax.experimental.pallas import tpu as pltpu
from jax.sharding import PartitionSpec as P

MESH = pl.DeviceIdType.MESH
BF = jnp.bfloat16
F32 = jnp.float32
HD = 128
SCALE = HD ** (-0.5)
LOG2E = math.log2(math.e)
BIG = 1e30
NEAR = (0, 1, 7, 2, 6, 3, 5, 4)
FAR = (4, 3, 5, 2, 6, 1, 7, 0)


def coords():
    b = lax.axis_index("blk")
    r = lax.axis_index("rep")
    x = b // 32
    y = b % 4
    z = (r // 2) * 8 + (b // 4) % 8
    return x, y, z, r % 2


def dev(x, y, z, c):
    xx = (x + 4) % 4
    yy = (y + 4) % 4
    zz = (z + 16) % 16
    return ((xx * 8 + zz % 8) * 4 + yy, (zz // 8) * 2 + c)


def zoff(s, c):
    return (s + 3 + c) % 8 - 3 - c


def entry_barrier(x, y, z, c):
    group = [dev(x, y, z, 1 - c)]
    for d in (1, 2, 3):
        group.append(dev(x + d, y, z, c))
        group.append(dev(x, y + d, z, c))
    for o in (1, 2, 3, 4, -1, -2, -3, -4):
        group.append(dev(x, y, z + o, c))
    barrier = pltpu.get_barrier_semaphore()
    for d in group:
        pl.semaphore_signal(barrier, inc=1, device_id=d, device_id_type=MESH)
    return barrier, len(group)


def rcopy(src, dst, ssem, rsem, device):
    return pltpu.make_async_remote_copy(
        src_ref=src, dst_ref=dst, send_sem=ssem, recv_sem=rsem, device_id=device, device_id_type=MESH
    )


def nt(a, b):
    return lax.dot_general(a, b, (((1,), (1,)), ((), ())), preferred_element_type=F32)


def nn(a, b):
    return lax.dot_general(a, b, (((1,), (0,)), ((), ())), preferred_element_type=F32)


def prepare_rows(sm_ref, rw):
    sel = lax.broadcasted_iota(jnp.int32, (1, HD), 1) < 64
    for i in range(4):
        t = sm_ref[i]
        tr = pltpu.roll(t, 64, 1)
        cs = pl.ds(i * HD, HD)
        lse = t[0:2] * LOG2E
        lser = tr[0:2] * LOG2E
        rw[0:1, cs] = jnp.where(sel, lse[0:1], lser[1:2])
        rw[1:2, cs] = jnp.where(sel, lser[0:1], lse[1:2])
        rw[2:3, cs] = jnp.where(sel, t[2:3], tr[3:4]) * SCALE
        rw[3:4, cs] = jnp.where(sel, tr[2:3], t[3:4]) * SCALE
        rw[4:6, cs] = jnp.broadcast_to(t[4:6, 0:1], (2, HD))


def key_half(s, kh, qx, rw, kv_ref, kp_ref, dkv, dqt):
    rows = pl.ds(64 * kh, 64)
    kc = kv_ref[0, s, :, rows, :].reshape(256, HD)
    vc = kv_ref[1, s, :, rows, :].reshape(256, HD)
    kt = kc.T
    dk = jnp.zeros((256, HD), F32)
    dv = jnp.zeros((256, HD), F32)
    for half in ((0, 1) if kh == 0 else (1,)):
        for g in range(2):
            ls = pl.ds(256 * g, 256)
            lse = rw[half : half + 1, ls]
            dlt = rw[2 + half : 3 + half, ls]
            if kh != half:
                le = jnp.broadcast_to(lse, (4, 256))
            else:
                qp = rw[4:5, ls].astype(jnp.int32) * 32768 + rw[5:6, ls].astype(jnp.int32)
                parts = []
                for yb in range(4):
                    kp = jnp.broadcast_to(kp_ref[yb, s][:, 0:1], (1, 256))
                    seen = kp <= qp if kh == 0 else kp >= qp
                    parts.append(jnp.where(seen, lse, BIG))
                le = jnp.concatenate(parts, axis=0)
            qg = qx[0, half, 2 * g : 2 * g + 2].reshape(256, HD)
            dg = qx[1, half, 2 * g : 2 * g + 2].reshape(256, HD)
            sc = nt(kc, qg).reshape(4, 64, 256)
            dp = nt(vc, dg)
            t = (sc * (SCALE * LOG2E) - le[:, None, :]).reshape(256, 256)
            if kh == half and g == 0:
                ri = lax.broadcasted_iota(jnp.int32, (64, HD), 0)
                li = lax.broadcasted_iota(jnp.int32, (64, HD), 1)
                own = jnp.where(ri <= li % 64 + 64 * s, t[:64, :HD], -BIG)
                t = jnp.concatenate([jnp.concatenate([own, t[:64, HD:]], axis=1), t[64:]], axis=0)
            p = jnp.exp2(t)
            ds = (p * (dp * SCALE - dlt)).astype(BF)
            dv = dv + nn(p.astype(BF), dg)
            dk = dk + nn(ds, qg)
            dqt[half, :, ls] += nn(kt, ds)
    dkv[s, 0, :, rows, :] = dk.reshape(4, 64, HD)
    dkv[s, 1, :, rows, :] = dv.reshape(4, 64, HD)


def fused_kernel(
    q_ref, k_ref, v_ref, o_ref, do_ref, lse_ref, pos_ref,
    gq_ref, gk_ref, gv_ref,
    qx, sm, kv, kp, rw, dqt, dkv, so, sib, acc, fa, fb, ra, rb, rc, zb, zin, tot0, dqs, qin, fin, qfin,
    zs, zr, pzs, pzr, ys, yr, kys, kyr, bs, br, xs, xr, ms, mr,
    rbs, rbr, rys, ryr, rzs, rzr, rxs, rxr, fs, fr,
):
    x, y, z, c = coords()
    barrier, count = entry_barrier(x, y, z, c)
    other = dev(x, y, z, 1 - c)
    up, down = dev(x, y + 1, z, c), dev(x, y - 1, z, c)
    right, left = dev(x + 1, y, z, c), dev(x - 1, y, z, c)
    top, bot = pl.ds(0, 64), pl.ds(64, 64)
    rest = pl.ds(1, 3)
    col = pl.multiple_of(c * 256, 256)

    for h in range(2):
        for half in range(2):
            for n, ref in ((0, q_ref), (1, do_ref)):
                qx[n, half, 0, pl.ds(64 * h, 64), :] = ref[pl.ds(64 * half, 64), pl.ds(col + HD * h, HD)]
    kv[0, 0, 0] = k_ref[...]
    kv[1, 0, 0] = v_ref[...]
    kp[0, 0] = pos_ref[...]
    rows = []
    for h in range(2):
        rows.append(lse_ref[pl.ds(2 * c + h, 1), :])
    for h in range(2):
        prod = do_ref[:, pl.ds(col + h * HD, HD)].astype(F32) * o_ref[:, pl.ds(col + h * HD, HD)].astype(F32)
        total = jnp.sum(prod, axis=1, keepdims=True)
        rows.append(jnp.broadcast_to(total, (HD, HD)).T[0:1, :])
    p = pos_ref[...]
    rows.append((p // 32768).astype(F32))
    rows.append((p % 32768).astype(F32))
    rows.append(jnp.zeros((2, HD), F32))
    sm[0] = jnp.concatenate(rows, axis=0)
    pl.semaphore_wait(barrier, count)

    def z_copy(s):
        return rcopy(kv.at[c, 0, 0], kv.at[c, s, 0], zs.at[s], zr.at[s], dev(x, y, z - zoff(s, c), c))

    def pz_copy(s):
        return rcopy(kp.at[0, 0], kp.at[0, s], pzs.at[s], pzr.at[s], dev(x, y, z - zoff(s, c), c))

    def ky_copy(s, d):
        return rcopy(kp.at[0, s], kp.at[d, s], kys.at[s, d], kyr.at[s, d], dev(x, y - d, z, c))

    def full_up(s):
        return rcopy(kv.at[c, s, 0], kv.at[c, s, 3], ys.at[s, 0], yr.at[s, 0], up)

    def full_down(s):
        return rcopy(kv.at[c, s, 0], kv.at[c, s, 1], ys.at[s, 1], yr.at[s, 1], down)

    def half_up(s):
        return rcopy(kv.at[c, s, 3, top], kv.at[c, s, 2, top], ys.at[s, 2], yr.at[s, 2], up)

    def half_down(s):
        return rcopy(kv.at[c, s, 1, bot], kv.at[c, s, 2, bot], ys.at[s, 3], yr.at[s, 3], down)

    opp0 = rcopy(kv.at[c, 0, 0], kv.at[c, 0, 2], ys.at[0, 2], yr.at[0, 2], dev(x, y + 2, z, c))

    def sib_own(s, kind):
        return rcopy(kv.at[kind, s, 0], kv.at[kind, s, 0], bs.at[s, 0], br.at[s, 0], other)

    def sib_rest(s, kind):
        return rcopy(kv.at[kind, s, rest], kv.at[kind, s, rest], bs.at[s, 1], br.at[s, 1], other)

    def x_copy(n):
        src, dst, half, to = (
            (0, 3, 0, right), (0, 3, 1, right), (0, 1, 1, left), (0, 1, 0, left), (3, 2, 0, right), (1, 2, 1, left)
        )[n]
        return rcopy(qx.at[:, half, src], qx.at[:, half, dst], xs.at[n], xr.at[n], to)

    def m_copy(d):
        return rcopy(sm.at[0], sm.at[d], ms.at[d], mr.at[d], dev(x - d, y, z, c))

    def stage_full(s):
        z_copy(s).wait_recv()
        full_up(s).start()
        full_down(s).start()
        sib_own(s, c).start()
        pz_copy(s).wait_recv()
        for d in (1, 2, 3):
            ky_copy(s, d).start()

    def stage_half(s):
        full_up(s).wait_recv()
        half_up(s).start()
        full_down(s).wait_recv()
        half_down(s).start()

    def stage_sib(s):
        half_up(s).wait_recv()
        half_down(s).wait_recv()
        sib_rest(s, c).start()

    def rs_copy(s):
        return rcopy(so.at[s], sib.at[s], rbs.at[s], rbr.at[s], other)

    def ra_top(s):
        return rcopy(acc.at[s, 2, top], fa.at[s], rys.at[s, 0], ryr.at[s, 0], up)

    def ra_bot(s):
        return rcopy(acc.at[s, 2, bot], fb.at[s], rys.at[s, 1], ryr.at[s, 1], down)

    def rb_up(s):
        return rcopy(acc.at[s, 1], ra.at[s], rys.at[s, 2], ryr.at[s, 2], up)

    def rb_down(s):
        return rcopy(acc.at[s, 3], rb.at[s], rys.at[s, 3], ryr.at[s, 3], down)

    opp7 = rcopy(acc.at[7, 2], rc, rys.at[7, 0], ryr.at[7, 0], dev(x, y + 2, z, c))

    def rz_copy(s):
        return rcopy(zb.at[s], zin.at[s], rzs.at[s], rzr.at[s], dev(x, y, z + zoff(s, c), c))

    def rx_copy(d):
        return rcopy(dqs.at[d], qin.at[d], rxs.at[d], rxr.at[d], dev(x + d, y, z, c))

    def presum(s):
        rs_copy(s).wait_recv()
        for d in (2, 1, 3):
            acc[s, d] = (dkv[s, c, d] + sib[s, d].astype(F32)).astype(BF)

    def stage_a(s):
        presum(s)
        ra_top(s).start()
        ra_bot(s).start()

    def stage_b(s):
        ra_top(s).wait_recv()
        acc[s, 1, top] = (acc[s, 1, top].astype(F32) + fa[s].astype(F32)).astype(BF)
        rb_up(s).start()
        ra_bot(s).wait_recv()
        acc[s, 3, bot] = (acc[s, 3, bot].astype(F32) + fb[s].astype(F32)).astype(BF)
        rb_down(s).start()

    def own_sum(s):
        rb_up(s).wait_recv()
        rb_down(s).wait_recv()
        return dkv[s, c, 0] + sib[s, 0].astype(F32) + ra[s].astype(F32) + rb[s].astype(F32)

    full_up(0).start()
    full_down(0).start()
    opp0.start()
    for s in range(1, 8):
        z_copy(s).start()
    for n in range(4):
        x_copy(n).start()
    for d in (1, 2, 3):
        m_copy(d).start()
        ky_copy(0, d).start()
    for s in range(1, 8):
        pz_copy(s).start()
    dqt[...] = jnp.zeros_like(dqt)
    stage_full(1)
    full_up(0).wait_recv()
    full_down(0).wait_recv()
    opp0.wait_recv()
    sib_rest(0, c).start()
    x_copy(0).wait_recv()
    x_copy(4).start()
    x_copy(2).wait_recv()
    x_copy(5).start()
    stage_full(2)
    stage_half(1)
    stage_full(3)
    for d in (1, 2, 3):
        m_copy(d).wait_recv()
    prepare_rows(sm, rw)
    for n in (1, 3, 4, 5):
        x_copy(n).wait_recv()

    def slot(s, carry):
        @pl.when(s < 4)
        def _():
            stage_full(s + 4)

        @pl.when(s < 6)
        def _():
            stage_half(s + 2)

        @pl.when(s < 7)
        def _():
            stage_sib(s + 1)

        @pl.when(s > 0)
        def _():
            sib_own(s, 1 - c).wait_recv()

        sib_rest(s, 1 - c).wait_recv()
        for d in (1, 2, 3):
            ky_copy(s, d).wait_recv()
        key_half(s, 0, qx, rw, kv, kp, dkv, dqt)

        @pl.when(s > 0)
        def _():
            stage_a(s - 1)

        @pl.when(s > 1)
        def _():
            stage_b(s - 2)

        @pl.when(s == 3)
        def _():
            tot0[...] = own_sum(0)

        @pl.when(s > 3)
        def _():
            zb[s - 3] = own_sum(s - 3).astype(BF)
            rz_copy(s - 3).start()

        key_half(s, 1, qx, rw, kv, kp, dkv, dqt)
        so[s] = dkv[s, 1 - c].astype(BF)
        rs_copy(s).start()
        return carry

    lax.fori_loop(0, 8, slot, 0)
    for i in (2, 1, 3, 0):
        for half in range(2):
            tile = dqt[half, :, pl.ds(i * HD, HD)].T.astype(BF)
            for h in range(2):
                dqs[i, pl.ds(64 * half, 64), pl.ds(HD * h, HD)] = tile[64 * h : 64 * h + 64]
        if i:
            rx_copy(i).start()
    presum(7)
    opp7.start()
    rb_up(7).start()
    rb_down(7).start()
    stage_b(6)

    def to_owner(s):
        zb[s] = own_sum(s).astype(BF)
        rz_copy(s).start()

    to_owner(5)
    opp7.wait_recv()
    zb[7] = (own_sum(7) + rc[...].astype(F32)).astype(BF)
    rz_copy(7).start()
    to_owner(6)
    qsum = dqs[0].astype(F32)
    for d in (1, 3, 2):
        rx_copy(d).wait_recv()
        qsum = qsum + qin[d].astype(F32)
    qfin[0] = qsum.astype(BF)
    sq = rcopy(qfin.at[0], qfin.at[1], fs.at[0], fr.at[0], other)
    sq.start()
    tot = tot0[...]
    for s in range(1, 8):
        rz_copy(s).wait_recv()
        tot = tot + zin[s].astype(F32)
    fin[0] = tot.astype(BF)
    sk = rcopy(fin.at[0], fin.at[1], fs.at[1], fr.at[1], other)
    sk.start()
    low = c == 0
    sq.wait_recv()
    gq_ref[:, 0:256] = jnp.where(low, qfin[0], qfin[1])
    gq_ref[:, 256:512] = jnp.where(low, qfin[1], qfin[0])
    for n in range(6):
        x_copy(n).wait_send()
    for d in (1, 2, 3):
        m_copy(d).wait_send()
        rx_copy(d).wait_send()
    full_up(0).wait_send()
    full_down(0).wait_send()
    opp0.wait_send()
    sib_rest(0, c).wait_send()
    rs_copy(0).wait_send()
    for d in (1, 2, 3):
        ky_copy(0, d).wait_send()
    opp7.wait_send()
    ra_top(0).wait_send()
    ra_bot(0).wait_send()
    rb_up(0).wait_send()
    rb_down(0).wait_send()

    def drain(s, carry):
        z_copy(s).wait_send()
        pz_copy(s).wait_send()
        full_up(s).wait_send()
        full_down(s).wait_send()
        half_up(s).wait_send()
        half_down(s).wait_send()
        sib_own(s, c).wait_send()
        sib_rest(s, c).wait_send()
        for d in (1, 2, 3):
            ky_copy(s, d).wait_send()
        rs_copy(s).wait_send()
        rb_up(s).wait_send()
        rb_down(s).wait_send()
        rz_copy(s).wait_send()

        @pl.when(s < 7)
        def _():
            ra_top(s).wait_send()
            ra_bot(s).wait_send()

        return carry

    lax.fori_loop(1, 8, drain, 0)
    sq.wait_send()
    sk.wait()
    gk_ref[...] = jnp.where(low, fin[0], fin[1])
    gv_ref[...] = jnp.where(low, fin[1], fin[0])


VM = pl.BlockSpec(memory_space=pltpu.VMEM)
DMA = pltpu.SemaphoreType.DMA


def per_device(queries, keys, values, output, grad_out, lse, positions):
    return pl.pallas_call(
        fused_kernel,
        out_shape=(
            jax.ShapeDtypeStruct((128, 512), BF),
            jax.ShapeDtypeStruct((128, 128), BF),
            jax.ShapeDtypeStruct((128, 128), BF),
        ),
        in_specs=[VM] * 7,
        out_specs=(VM,) * 3,
        scratch_shapes=[
            pltpu.VMEM((2, 2, 4, 128, 128), BF),
            pltpu.VMEM((4, 8, 128), F32),
            pltpu.VMEM((2, 8, 4, 128, 128), BF),
            pltpu.VMEM((4, 8, 1, 128), jnp.int32),
            pltpu.VMEM((8, 512), F32),
            pltpu.VMEM((2, 128, 512), F32),
            pltpu.VMEM((8, 2, 4, 128, 128), F32),
            pltpu.VMEM((8, 4, 128, 128), BF),
            pltpu.VMEM((8, 4, 128, 128), BF),
            pltpu.VMEM((8, 4, 128, 128), BF),
            pltpu.VMEM((8, 64, 128), BF),
            pltpu.VMEM((8, 64, 128), BF),
            pltpu.VMEM((8, 128, 128), BF),
            pltpu.VMEM((8, 128, 128), BF),
            pltpu.VMEM((128, 128), BF),
            pltpu.VMEM((8, 128, 128), BF),
            pltpu.VMEM((8, 128, 128), BF),
            pltpu.VMEM((128, 128), F32),
            pltpu.VMEM((4, 128, 256), BF),
            pltpu.VMEM((4, 128, 256), BF),
            pltpu.VMEM((2, 128, 128), BF),
            pltpu.VMEM((2, 128, 256), BF),
            DMA((8,)), DMA((8,)), DMA((8,)), DMA((8,)), DMA((8, 4)), DMA((8, 4)), DMA((8, 4)), DMA((8, 4)),
            DMA((8, 2)), DMA((8, 2)), DMA((6,)), DMA((6,)), DMA((4,)), DMA((4,)),
            DMA((8,)), DMA((8,)), DMA((8, 4)), DMA((8, 4)), DMA((8,)), DMA((8,)), DMA((4,)), DMA((4,)),
            DMA((2,)), DMA((2,)),
        ],
        compiler_params=pltpu.CompilerParams(collective_id=0, has_side_effects=True),
        name="attention_grad",
    )(queries, keys, values, output, grad_out, lse, positions.reshape(1, 128))


def solution(mesh):
    placed = (
        P("blk", None),
        P("blk", None),
        P("blk", None),
        P("blk", None),
        P("blk", None),
        P(None, "blk"),
        P("blk"),
    )
    return jax.shard_map(
        per_device,
        mesh=mesh,
        in_specs=placed,
        out_specs=(P("blk", None), P("blk", None), P("blk", None)),
        check_vma=False,
    )
```

```python
import math

import jax
import jax.numpy as jnp
from jax import lax
from jax.experimental import pallas as pl
from jax.experimental.pallas import tpu as pltpu
from jax.sharding import PartitionSpec as P

MESH = pl.DeviceIdType.MESH
BF = jnp.bfloat16
F32 = jnp.float32
HD = 128
SCALE = HD ** (-0.5)
LOG2E = math.log2(math.e)
BIG = 1e30
DIRECT = 5


def coords():
    b = lax.axis_index("blk")
    r = lax.axis_index("rep")
    x = b // 32
    y = b % 4
    z = (r // 2) * 8 + (b // 4) % 8
    return x, y, z, r % 2


def dev(x, y, z, c):
    xx = (x + 4) % 4
    yy = (y + 4) % 4
    zz = (z + 16) % 16
    return ((xx * 8 + zz % 8) * 4 + yy, (zz // 8) * 2 + c)


def zoff(s, c):
    return (s + 3 + c) % 8 - 3 - c


def entry_barrier(x, y, z, c):
    group = [dev(x, y, z, 1 - c)]
    for d in (1, 2, 3):
        group.append(dev(x + d, y, z, c))
        group.append(dev(x, y + d, z, c))
    for o in (1, 2, 3, 4, -1, -2, -3, -4):
        group.append(dev(x, y, z + o, c))
    barrier = pltpu.get_barrier_semaphore()
    for d in group:
        pl.semaphore_signal(barrier, inc=1, device_id=d, device_id_type=MESH)
    return barrier, len(group)


def rcopy(src, dst, ssem, rsem, device):
    return pltpu.make_async_remote_copy(
        src_ref=src, dst_ref=dst, send_sem=ssem, recv_sem=rsem, device_id=device, device_id_type=MESH
    )


def nt(a, b):
    return lax.dot_general(a, b, (((1,), (1,)), ((), ())), preferred_element_type=F32)


def nn(a, b):
    return lax.dot_general(a, b, (((1,), (0,)), ((), ())), preferred_element_type=F32)


def prepare_rows(sm_ref, rw):
    sel = lax.broadcasted_iota(jnp.int32, (1, HD), 1) < 64
    for i in range(4):
        t = sm_ref[i]
        tr = pltpu.roll(t, 64, 1)
        cs = pl.ds(i * HD, HD)
        lse = t[0:2] * LOG2E
        lser = tr[0:2] * LOG2E
        rw[0:1, cs] = jnp.where(sel, lse[0:1], lser[1:2])
        rw[1:2, cs] = jnp.where(sel, lser[0:1], lse[1:2])
        rw[2:3, cs] = jnp.where(sel, t[2:3], tr[3:4]) * SCALE
        rw[3:4, cs] = jnp.where(sel, tr[2:3], t[3:4]) * SCALE
        rw[4:6, cs] = jnp.broadcast_to(t[4:6, 0:1], (2, HD))


def key_half(s, kh, qx, rw, kv_ref, kp_ref, dkv, dqt):
    rows = pl.ds(64 * kh, 64)
    kc = kv_ref[0, s, :, rows, :].reshape(256, HD)
    vc = kv_ref[1, s, :, rows, :].reshape(256, HD)
    kt = kc.T
    dk = jnp.zeros((256, HD), F32)
    dv = jnp.zeros((256, HD), F32)
    for half in ((0, 1) if kh == 0 else (1,)):
        for g in range(2):
            ls = pl.ds(256 * g, 256)
            lse = rw[half : half + 1, ls]
            dlt = rw[2 + half : 3 + half, ls]
            if kh != half:
                le = jnp.broadcast_to(lse, (4, 256))
            else:
                qp = rw[4:5, ls].astype(jnp.int32) * 32768 + rw[5:6, ls].astype(jnp.int32)
                parts = []
                for yb in range(4):
                    kp = jnp.broadcast_to(kp_ref[yb, s][:, 0:1], (1, 256))
                    seen = kp <= qp if kh == 0 else kp >= qp
                    parts.append(jnp.where(seen, lse, BIG))
                le = jnp.concatenate(parts, axis=0)
            qg = qx[0, half, 2 * g : 2 * g + 2].reshape(256, HD)
            dg = qx[1, half, 2 * g : 2 * g + 2].reshape(256, HD)
            sc = nt(kc, qg).reshape(4, 64, 256)
            dp = nt(vc, dg)
            t = (sc * (SCALE * LOG2E) - le[:, None, :]).reshape(256, 256)
            if kh == half and g == 0:
                ri = lax.broadcasted_iota(jnp.int32, (64, HD), 0)
                li = lax.broadcasted_iota(jnp.int32, (64, HD), 1)
                own = jnp.where(ri <= li % 64 + 64 * s, t[:64, :HD], -BIG)
                t = jnp.concatenate([jnp.concatenate([own, t[:64, HD:]], axis=1), t[64:]], axis=0)
            p = jnp.exp2(t)
            ds = (p * (dp * SCALE - dlt)).astype(BF)
            dv = dv + nn(p.astype(BF), dg)
            dk = dk + nn(ds, qg)
            dqt[half, :, ls] += nn(kt, ds)
    dkv[s, 0, :, rows, :] = dk.reshape(4, 64, HD)
    dkv[s, 1, :, rows, :] = dv.reshape(4, 64, HD)


def fused_kernel(
    q_ref, k_ref, v_ref, o_ref, do_ref, lse_ref, pos_ref,
    gq_ref, gk_ref, gv_ref,
    qx, sm, kv, kp, rw, dqt, dkv, so, sib, acc, fa, fb, ra, rb, rc, zb, zin, tot0, dqs, qin, fin, qfin,
    ss, zr, yr, br, xr, cr, rbr, ryr,
):
    x, y, z, c = coords()
    barrier, count = entry_barrier(x, y, z, c)
    other = dev(x, y, z, 1 - c)
    up, down = dev(x, y + 1, z, c), dev(x, y - 1, z, c)
    right, left = dev(x + 1, y, z, c), dev(x - 1, y, z, c)
    top, bot = pl.ds(0, 64), pl.ds(64, 64)
    rest = pl.ds(1, 3)
    col = pl.multiple_of(c * 256, 256)

    for h in range(2):
        for half in range(2):
            for n, ref in ((0, q_ref), (1, do_ref)):
                qx[n, half, 0, pl.ds(64 * h, 64), :] = ref[pl.ds(64 * half, 64), pl.ds(col + HD * h, HD)]
    kv[0, 0, 0] = k_ref[...]
    kv[1, 0, 0] = v_ref[...]
    kp[0, 0] = pos_ref[...]
    rows = []
    for h in range(2):
        rows.append(lse_ref[pl.ds(2 * c + h, 1), :])
    for h in range(2):
        prod = do_ref[:, pl.ds(col + h * HD, HD)].astype(F32) * o_ref[:, pl.ds(col + h * HD, HD)].astype(F32)
        total = jnp.sum(prod, axis=1, keepdims=True)
        rows.append(jnp.broadcast_to(total, (HD, HD)).T[0:1, :])
    p = pos_ref[...]
    rows.append((p // 32768).astype(F32))
    rows.append((p % 32768).astype(F32))
    rows.append(jnp.zeros((2, HD), F32))
    sm[0] = jnp.concatenate(rows, axis=0)
    pl.semaphore_wait(barrier, count)

    def z_copy(s):
        return rcopy(kv.at[c, 0, 0], kv.at[c, s, 0], ss.at[0], zr.at[s], dev(x, y, z - zoff(s, c), c))

    def pz_copy(s):
        return rcopy(kp.at[0, 0], kp.at[0, s], ss.at[1], cr.at[0], dev(x, y, z - zoff(s, c), c))

    def ky_copy(d):
        return rcopy(kp.at[0], kp.at[d], ss.at[2], cr.at[1], dev(x, y - d, z, c))

    def full_up(s):
        return rcopy(kv.at[c, s, 0], kv.at[c, s, 3], ss.at[3], yr.at[s, 0], up)

    def full_down(s):
        return rcopy(kv.at[c, s, 0], kv.at[c, s, 1], ss.at[4], yr.at[s, 1], down)

    def half_up(s):
        return rcopy(kv.at[c, s, 3, top], kv.at[c, s, 2, top], ss.at[5], yr.at[s, 2], up)

    def half_down(s):
        return rcopy(kv.at[c, s, 1, bot], kv.at[c, s, 2, bot], ss.at[6], yr.at[s, 3], down)

    opp0 = rcopy(kv.at[c, 0, 0], kv.at[c, 0, 2], ss.at[7], yr.at[0, 2], dev(x, y + 2, z, c))

    def sib_own(s):
        return rcopy(kv.at[c, s, 0], kv.at[c, s, 0], ss.at[8], br.at[s], other)

    def sib_rest(s):
        return rcopy(kv.at[c, s, rest], kv.at[c, s, rest], ss.at[9], br.at[s], other)

    def x_copy(n):
        src, dst, half, to = (
            (0, 3, 0, right), (0, 3, 1, right), (0, 1, 1, left), (0, 1, 0, left), (3, 2, 0, right), (1, 2, 1, left)
        )[n]
        return rcopy(qx.at[:, half, src], qx.at[:, half, dst], ss.at[10 + n], xr.at[n], to)

    def m_copy(d):
        return rcopy(sm.at[0], sm.at[d], ss.at[16], cr.at[2], dev(x - d, y, z, c))

    def stage_full(s):
        z_copy(s).wait_recv()
        full_up(s).start()
        full_down(s).start()
        sib_own(s).start()

    def stage_half(s):
        full_up(s).wait_recv()
        half_up(s).start()
        full_down(s).wait_recv()
        half_down(s).start()

    def stage_sib(s):
        half_up(s).wait_recv()
        half_down(s).wait_recv()
        sib_rest(s).start()

    def all_of(ref, sem):
        return pltpu.make_async_copy(ref, ref, sem)

    def rs_copy(s):
        return rcopy(so.at[s], sib.at[s], ss.at[17], rbr.at[s], other)

    def ra_top(s):
        return rcopy(acc.at[s, 2, top], fa.at[s], ss.at[18], ryr.at[s, 0], up)

    def ra_bot(s):
        return rcopy(acc.at[s, 2, bot], fb.at[s], ss.at[19], ryr.at[s, 1], down)

    def rb_up(s):
        return rcopy(acc.at[s, 1], ra.at[s], ss.at[20], ryr.at[s, 2], up)

    def rb_down(s):
        return rcopy(acc.at[s, 3], rb.at[s], ss.at[21], ryr.at[s, 3], down)

    def ro_copy(s):
        return rcopy(acc.at[s, 2], rc.at[s - DIRECT], ss.at[22], ryr.at[s, 0], dev(x, y + 2, z, c))

    def rz_copy(s):
        return rcopy(zb.at[s], zin.at[s], ss.at[23], cr.at[3], dev(x, y, z + zoff(s, c), c))

    def rx_copy(d, half):
        rows = pl.ds(64 * half, 64)
        return rcopy(dqs.at[d, rows], qin.at[d, rows], ss.at[24], cr.at[4], dev(x + d, y, z, c))

    def query_half(half):
        for i in (2, 1, 3, 0):
            tile = dqt[half, :, pl.ds(i * HD, HD)].T.astype(BF)
            for h in range(2):
                dqs[i, pl.ds(64 * half, 64), pl.ds(HD * h, HD)] = tile[64 * h : 64 * h + 64]
            if i:
                rx_copy(i, half).start()

    def presum(s):
        rs_copy(s).wait_recv()
        for d in (2, 1, 3):
            acc[s, d] = (dkv[s, c, d] + sib[s, d].astype(F32)).astype(BF)

    def stage_a(s):
        presum(s)
        ra_top(s).start()
        ra_bot(s).start()

    def stage_direct(s):
        presum(s)
        ro_copy(s).start()
        rb_up(s).start()
        rb_down(s).start()

    def stage_b(s):
        ra_top(s).wait_recv()
        acc[s, 1, top] = (acc[s, 1, top].astype(F32) + fa[s].astype(F32)).astype(BF)
        rb_up(s).start()
        ra_bot(s).wait_recv()
        acc[s, 3, bot] = (acc[s, 3, bot].astype(F32) + fb[s].astype(F32)).astype(BF)
        rb_down(s).start()

    def own_sum(s):
        rb_up(s).wait_recv()
        rb_down(s).wait_recv()
        return dkv[s, c, 0] + sib[s, 0].astype(F32) + ra[s].astype(F32) + rb[s].astype(F32)

    def to_owner(s, direct=False):
        t = own_sum(s)
        if direct:
            ro_copy(s).wait_recv()
            t = t + rc[s - DIRECT].astype(F32)
        zb[s] = t.astype(BF)
        rz_copy(s).start()

    full_up(0).start()
    full_down(0).start()
    opp0.start()
    for s in range(1, 8):
        pz_copy(s).start()
    for n in (0, 2, 1, 3):
        x_copy(n).start()
    for s in range(1, 8):
        z_copy(s).start()
    for d in (1, 2, 3):
        m_copy(d).start()
    dqt[...] = jnp.zeros_like(dqt)
    stage_full(1)
    full_up(0).wait_recv()
    full_down(0).wait_recv()
    opp0.wait_recv()
    sib_rest(0).start()
    x_copy(0).wait_recv()
    x_copy(4).start()
    x_copy(2).wait_recv()
    x_copy(5).start()
    stage_full(2)
    all_of(kp.at[0, pl.ds(1, 7)], cr.at[0]).wait()
    for d in (1, 2, 3):
        ky_copy(d).start()
    stage_full(3)
    stage_half(1)
    stage_full(4)
    stage_half(2)
    stage_full(5)
    all_of(sm.at[rest], cr.at[2]).wait()
    prepare_rows(sm, rw)
    for n in (1, 3, 4, 5):
        x_copy(n).wait_recv()
    stage_half(3)
    stage_sib(1)
    all_of(kp.at[rest], cr.at[1]).wait()

    def slot(s, carry):
        @pl.when(s < 2)
        def _():
            stage_full(s + 6)

        @pl.when(s < 4)
        def _():
            stage_half(s + 4)

        @pl.when((s >= 2) & (s < DIRECT + 2))
        def _():
            stage_a(s - 2)

        @pl.when(s >= DIRECT + 2)
        def _():
            stage_direct(s - 2)

        @pl.when(s >= 4)
        def _():
            stage_b(s - 4)

        @pl.when(s == 6)
        def _():
            tot0[...] = own_sum(0)

        @pl.when(s == 7)
        def _():
            to_owner(1)

        @pl.when(s > 0)
        def _():
            all_of(kv.at[1 - c, s], br.at[s]).wait()

        @pl.when(s == 0)
        def _():
            all_of(kv.at[1 - c, 0, rest], br.at[0]).wait()

        key_half(s, 0, qx, rw, kv, kp, dkv, dqt)

        @pl.when(s < 6)
        def _():
            stage_sib(s + 2)

        @pl.when(s == 7)
        def _():
            query_half(0)

        key_half(s, 1, qx, rw, kv, kp, dkv, dqt)
        so[s] = dkv[s, 1 - c].astype(BF)
        rs_copy(s).start()
        return carry

    lax.fori_loop(0, 8, slot, 0)
    query_half(1)
    stage_direct(6)
    stage_b(4)
    to_owner(2)
    to_owner(3)
    stage_direct(7)
    to_owner(5, True)
    to_owner(4)
    to_owner(6, True)
    all_of(kv.at[c, pl.ds(1, 7), 0], ss.at[0]).wait()
    all_of(kp.at[0, pl.ds(1, 7)], ss.at[1]).wait()
    all_of(kp.at[rest], ss.at[2]).wait()
    all_of(kv.at[c, :, 0], ss.at[3]).wait()
    all_of(kv.at[c, :, 0], ss.at[4]).wait()
    all_of(kv.at[c, pl.ds(1, 7), 2, top], ss.at[5]).wait()
    all_of(kv.at[c, pl.ds(1, 7), 2, bot], ss.at[6]).wait()
    opp0.wait_send()
    all_of(kv.at[c, pl.ds(1, 7), 0], ss.at[8]).wait()
    all_of(kv.at[c, :, rest], ss.at[9]).wait()
    for n in range(6):
        x_copy(n).wait_send()
    all_of(sm.at[rest], ss.at[16]).wait()
    to_owner(7, True)
    all_of(qin.at[rest], cr.at[4]).wait()
    qsum = dqs[0].astype(F32)
    for d in (1, 2, 3):
        qsum = qsum + qin[d].astype(F32)
    qfin[0] = qsum.astype(BF)
    sq = rcopy(qfin.at[0], qfin.at[1], ss.at[25], cr.at[5], other)
    sq.start()
    all_of(zin.at[pl.ds(1, 7)], cr.at[3]).wait()
    tot = tot0[...]
    for s in range(1, 8):
        tot = tot + zin[s].astype(F32)
    fin[0] = tot.astype(BF)
    sk = rcopy(fin.at[0], fin.at[1], ss.at[26], cr.at[6], other)
    sk.start()
    low = c == 0
    sq.wait_recv()
    gq_ref[:, 0:256] = jnp.where(low, qfin[0], qfin[1])
    gq_ref[:, 256:512] = jnp.where(low, qfin[1], qfin[0])
    all_of(sib, ss.at[17]).wait()
    all_of(fa.at[pl.ds(0, DIRECT)], ss.at[18]).wait()
    all_of(fb.at[pl.ds(0, DIRECT)], ss.at[19]).wait()
    all_of(ra, ss.at[20]).wait()
    all_of(rb, ss.at[21]).wait()
    all_of(rc, ss.at[22]).wait()
    all_of(zin.at[pl.ds(1, 7)], ss.at[23]).wait()
    all_of(qin.at[rest], ss.at[24]).wait()
    sq.wait_send()
    sk.wait()
    gk_ref[...] = jnp.where(low, fin[0], fin[1])
    gv_ref[...] = jnp.where(low, fin[1], fin[0])


VM = pl.BlockSpec(memory_space=pltpu.VMEM)
DMA = pltpu.SemaphoreType.DMA


def per_device(queries, keys, values, output, grad_out, lse, positions):
    return pl.pallas_call(
        fused_kernel,
        out_shape=(
            jax.ShapeDtypeStruct((128, 512), BF),
            jax.ShapeDtypeStruct((128, 128), BF),
            jax.ShapeDtypeStruct((128, 128), BF),
        ),
        in_specs=[VM] * 7,
        out_specs=(VM,) * 3,
        scratch_shapes=[
            pltpu.VMEM((2, 2, 4, 128, 128), BF),
            pltpu.VMEM((4, 8, 128), F32),
            pltpu.VMEM((2, 8, 4, 128, 128), BF),
            pltpu.VMEM((4, 8, 1, 128), jnp.int32),
            pltpu.VMEM((8, 512), F32),
            pltpu.VMEM((2, 128, 512), F32),
            pltpu.VMEM((8, 2, 4, 128, 128), F32),
            pltpu.VMEM((8, 4, 128, 128), BF),
            pltpu.VMEM((8, 4, 128, 128), BF),
            pltpu.VMEM((8, 4, 128, 128), BF),
            pltpu.VMEM((8, 64, 128), BF),
            pltpu.VMEM((8, 64, 128), BF),
            pltpu.VMEM((8, 128, 128), BF),
            pltpu.VMEM((8, 128, 128), BF),
            pltpu.VMEM((8 - DIRECT, 128, 128), BF),
            pltpu.VMEM((8, 128, 128), BF),
            pltpu.VMEM((8, 128, 128), BF),
            pltpu.VMEM((128, 128), F32),
            pltpu.VMEM((4, 128, 256), BF),
            pltpu.VMEM((4, 128, 256), BF),
            pltpu.VMEM((2, 128, 128), BF),
            pltpu.VMEM((2, 128, 256), BF),
            DMA((27,)), DMA((8,)), DMA((8, 4)), DMA((8,)), DMA((6,)), DMA((7,)), DMA((8,)), DMA((8, 4)),
        ],
        compiler_params=pltpu.CompilerParams(collective_id=0, has_side_effects=True),
        name="attention_grad",
    )(queries, keys, values, output, grad_out, lse, positions.reshape(1, 128))


def solution(mesh):
    placed = (
        P("blk", None),
        P("blk", None),
        P("blk", None),
        P("blk", None),
        P("blk", None),
        P(None, "blk"),
        P("blk"),
    )
    return jax.shard_map(
        per_device,
        mesh=mesh,
        in_specs=placed,
        out_specs=(P("blk", None), P("blk", None), P("blk", None)),
        check_vma=False,
    )
```

```python
import math

import jax
import jax.numpy as jnp
from jax import lax
from jax.experimental import pallas as pl
from jax.experimental.pallas import tpu as pltpu
from jax.sharding import PartitionSpec as P

MESH = pl.DeviceIdType.MESH
BF = jnp.bfloat16
F32 = jnp.float32
HD = 128
SCALE = HD ** (-0.5)
LOG2E = math.log2(math.e)
BIG = 1e30


def coords():
    b = lax.axis_index("blk")
    r = lax.axis_index("rep")
    x = b // 32
    y = b % 4
    z = (r // 2) * 8 + (b // 4) % 8
    return x, y, z, r % 2


def dev(x, y, z, c):
    xx = (x + 4) % 4
    yy = (y + 4) % 4
    zz = (z + 16) % 16
    return ((xx * 8 + zz % 8) * 4 + yy, (zz // 8) * 2 + c)


def entry_barrier(x, y, z, c):
    group = [dev(x, y, z, 1 - c)]
    for d in (1, 2, 3):
        group.append(dev(x + d, y, z, c))
        group.append(dev(x, y + d, z, c))
    for o in (1, 2, 3, -1, -2, -3):
        group.append(dev(x, y, z + o, c))
    barrier = pltpu.get_barrier_semaphore()
    for d in group:
        pl.semaphore_signal(barrier, inc=1, device_id=d, device_id_type=MESH)
    return barrier, len(group)


def rcopy(src, dst, ssem, rsem, device):
    return pltpu.make_async_remote_copy(
        src_ref=src, dst_ref=dst, send_sem=ssem, recv_sem=rsem, device_id=device, device_id_type=MESH
    )


def nt(a, b):
    return lax.dot_general(a, b, (((1,), (1,)), ((), ())), preferred_element_type=F32)


def nn(a, b):
    return lax.dot_general(a, b, (((1,), (0,)), ((), ())), preferred_element_type=F32)


def prepare_rows(sm_ref, rw, blocks):
    for i in blocks:
        rw[:, pl.ds(i * HD, HD)] = sm_ref[i]


def key_half(s, kh, u, qx, rw, kv_ref, kp_ref, dkv, dqt):
    rows = pl.ds(64 * kh, 64)
    kc = kv_ref[0, s, :, rows, :].reshape(256, HD)
    vc = kv_ref[1, s, :, rows, :].reshape(256, HD)
    kt = kc.T
    dk = jnp.zeros((256, HD), F32)
    dv = jnp.zeros((256, HD), F32)
    for half in ((0, 1) if kh == 0 else (1,)):
        for g in (2 * u, 2 * u + 1):
            ls = pl.ds(256 * g, 256)
            lse = rw[half : half + 1, ls]
            dlt = rw[2 + half : 3 + half, ls]
            if kh != half:
                le = jnp.broadcast_to(lse, (4, 256))
            else:
                qp = rw[4:5, ls].astype(jnp.int32) * 32768 + rw[5:6, ls].astype(jnp.int32)
                parts = []
                for yb in range(4):
                    kp = jnp.broadcast_to(kp_ref[yb, s][:, 0:1], (1, 256))
                    seen = kp <= qp if kh == 0 else kp >= qp
                    parts.append(jnp.where(seen, lse, BIG))
                le = jnp.concatenate(parts, axis=0)
            qg = qx[0, half, 2 * g : 2 * g + 2].reshape(256, HD)
            dg = qx[1, half, 2 * g : 2 * g + 2].reshape(256, HD)
            sc = nt(kc, qg).reshape(4, 64, 256)
            dp = nt(vc, dg)
            t = (sc * (SCALE * LOG2E) - le[:, None, :]).reshape(256, 256)
            if kh == half and g == 0:
                ri = lax.broadcasted_iota(jnp.int32, (64, HD), 0)
                li = lax.broadcasted_iota(jnp.int32, (64, HD), 1)
                own = jnp.where(ri <= li % 64 + 64 * s, t[:64, :HD], -BIG)
                t = jnp.concatenate([jnp.concatenate([own, t[:64, HD:]], axis=1), t[64:]], axis=0)
            p = jnp.exp2(t)
            ds = (p * (dp * SCALE - dlt)).astype(BF)
            dv = dv + nn(p.astype(BF), dg)
            dk = dk + nn(ds, qg)
            dqt[half, :, ls] += nn(kt, ds)
    if u:
        dk = dk + dkv[s, 0, :, rows, :].reshape(256, HD)
        dv = dv + dkv[s, 1, :, rows, :].reshape(256, HD)
    dkv[s, 0, :, rows, :] = dk.reshape(4, 64, HD)
    dkv[s, 1, :, rows, :] = dv.reshape(4, 64, HD)


def fused_kernel(
    q_ref, k_ref, v_ref, o_ref, do_ref, lse_ref, pos_ref,
    gq_ref, gk_ref, gv_ref,
    qx, sm, kv, kp, rw, dqt, dkv, so, sib, acc, fa, fb, ra, rb, rc, zb, zin, tot0, dqs, qin, qb, qp, fin, qfin,
    ov, lv, pv, ss, zr, yr, br, xr, cr, rbr, ryr, ir,
):
    x, y, z, c = coords()
    barrier, count = entry_barrier(x, y, z, c)
    other = dev(x, y, z, 1 - c)
    up, down = dev(x, y + 1, z, c), dev(x, y - 1, z, c)
    right, left = dev(x + 1, y, z, c), dev(x - 1, y, z, c)
    away = 2 * (z % 2) - 1
    partner = dev(x, y, z - away, c)
    top, bot = pl.ds(0, 64), pl.ds(64, 64)
    rest = pl.ds(1, 3)
    col = pl.multiple_of(c * 256, 256)

    def all_of(ref, sem):
        return pltpu.make_async_copy(ref, ref, sem)

    pltpu.make_async_copy(k_ref, kv.at[0, 0, 0], ir.at[0]).start()
    pltpu.make_async_copy(v_ref, kv.at[1, 0, 0], ir.at[1]).start()
    for n, ref, dst in ((2, do_ref, qx.at[1, :, 0]), (3, o_ref, ov), (4, q_ref, qx.at[0, :, 0])):
        for half in range(2):
            for h in range(2):
                pltpu.make_async_copy(
                    ref.at[pl.ds(64 * half, 64), pl.ds(col + HD * h, HD)], dst.at[half, pl.ds(64 * h, 64)], ir.at[n]
                ).start()
    pltpu.make_async_copy(lse_ref, lv, ir.at[5]).start()
    pltpu.make_async_copy(pos_ref, pv, ir.at[6]).start()
    all_of(qx.at[1, :, 0], ir.at[2]).wait()
    all_of(ov, ir.at[3]).wait()
    all_of(lv, ir.at[5]).wait()
    all_of(pv, ir.at[6]).wait()
    sel = lax.broadcasted_iota(jnp.int32, (1, HD), 1) < 64
    l0 = lv[pl.ds(2 * c, 1), :] * LOG2E
    l1 = lv[pl.ds(2 * c + 1, 1), :] * LOG2E
    rows = [jnp.where(sel, l0, pltpu.roll(l1, 64, 1)), jnp.where(sel, pltpu.roll(l0, 64, 1), l1)]
    for half in range(2):
        prod = qx[1, half, 0].astype(F32) * ov[half].astype(F32)
        total = jnp.sum(prod, axis=1, keepdims=True) * SCALE
        rows.append(jnp.broadcast_to(total, (HD, HD)).T[0:1, :])
    p = jnp.broadcast_to(pv[0:1, 0:1], (1, HD))
    rows.append((p // 32768).astype(F32))
    rows.append((p % 32768).astype(F32))
    rows.append(jnp.zeros((2, HD), F32))
    sm[0] = jnp.concatenate(rows, axis=0)
    kp[0, 0] = pv[...]
    dqt[...] = jnp.zeros_like(dqt)
    all_of(kv.at[0, 0, 0], ir.at[0]).wait()
    all_of(kv.at[1, 0, 0], ir.at[1]).wait()
    all_of(qx.at[0, :, 0], ir.at[4]).wait()
    pl.semaphore_wait(barrier, count)

    def z_copy(s):
        to = z + s * away if s % 2 else z - s * away
        return rcopy(kv.at[c, 0, 0], kv.at[c, s, 0], ss.at[0], zr.at[s], dev(x, y, to, c))

    def pz_copy(s):
        to = z + s * away if s % 2 else z - s * away
        return rcopy(kp.at[0, 0], kp.at[0, s], ss.at[1], cr.at[0], dev(x, y, to, c))

    def ky_copy(d):
        return rcopy(kp.at[0], kp.at[d], ss.at[2], cr.at[1], dev(x, y - d, z, c))

    def full_up(s):
        return rcopy(kv.at[c, s, 0], kv.at[c, s, 3], ss.at[3], yr.at[s, 0], up)

    def full_down(s):
        return rcopy(kv.at[c, s, 0], kv.at[c, s, 1], ss.at[4], yr.at[s, 1], down)

    def half_up(s):
        return rcopy(kv.at[c, s, 3, top], kv.at[c, s, 2, top], ss.at[5], yr.at[s, 2], up)

    def half_down(s):
        return rcopy(kv.at[c, s, 1, bot], kv.at[c, s, 2, bot], ss.at[6], yr.at[s, 3], down)

    opp0 = rcopy(kv.at[c, 0, 0], kv.at[c, 0, 2], ss.at[7], yr.at[0, 2], dev(x, y + 2, z, c))

    def sib_own(s):
        return rcopy(kv.at[c, s, 0], kv.at[c, s, 0], ss.at[8], br.at[s], other)

    def sib_rest(s):
        return rcopy(kv.at[c, s, rest], kv.at[c, s, rest], ss.at[9], br.at[s], other)

    def x_copy(n, u):
        src, dst, half, to = (
            (0, 3, 0, right), (0, 3, 1, right), (0, 1, 1, left), (0, 1, 0, left), (3, 2, 0, right), (1, 2, 1, left)
        )[n]
        return rcopy(
            qx.at[:, half, src + 4 * u], qx.at[:, half, dst + 4 * u], ss.at[10 + n + 18 * u], xr.at[u, n], to
        )

    def zq_copy(half):
        return rcopy(qx.at[:, half, 0], qx.at[:, half, 4], ss.at[34], cr.at[8 + half], partner)

    def m_copy(d):
        return rcopy(sm.at[0], sm.at[d], ss.at[16], cr.at[2], dev(x - d, y, z, c))

    mz_copy = rcopy(sm.at[0], sm.at[4], ss.at[35], cr.at[10], partner)

    def m2_copy(d):
        return rcopy(sm.at[4], sm.at[4 + d], ss.at[36], cr.at[11], dev(x - d, y, z, c))

    def stage_full(s):
        z_copy(s).wait_recv()
        full_up(s).start()
        full_down(s).start()
        sib_own(s).start()

    def stage_half(s):
        full_up(s).wait_recv()
        half_up(s).start()
        full_down(s).wait_recv()
        half_down(s).start()

    def stage_sib(s):
        half_up(s).wait_recv()
        half_down(s).wait_recv()
        sib_rest(s).start()

    def rs_copy(s):
        return rcopy(so.at[s], sib.at[s], ss.at[17], rbr.at[s], other)

    def ra_top(s):
        return rcopy(acc.at[s, 2, top], fa.at[s - 2], ss.at[18], ryr.at[s, 0], up)

    def ra_bot(s):
        return rcopy(acc.at[s, 2, bot], fb.at[s - 2], ss.at[19], ryr.at[s, 1], down)

    def rb_up(s):
        return rcopy(acc.at[s, 1], ra.at[s], ss.at[20], ryr.at[s, 2], up)

    def rb_down(s):
        return rcopy(acc.at[s, 3], rb.at[s], ss.at[21], ryr.at[s, 3], down)

    def ro_copy(s):
        return rcopy(acc.at[s, 2], rc.at[s], ss.at[22], ryr.at[s, 0], dev(x, y + 2, z, c))

    def rz_copy(s):
        return rcopy(zb.at[s], zin.at[s], ss.at[23], cr.at[3], dev(x, y, z + s * away, c))

    def rx_copy(d, half, u):
        rows = pl.ds(64 * half, 64)
        got = cr.at[12 + half] if u else cr.at[4]
        return rcopy(
            dqs.at[d + 4 * u, rows], qin.at[d + 4 * u, rows], ss.at[37 if u else 24], got, dev(x + d, y, z, c)
        )

    def rp_copy(half):
        rows = pl.ds(64 * half, 64)
        return rcopy(qb.at[rows], qp.at[rows], ss.at[38], cr.at[14 + half], partner)

    def share(half):
        rows = pl.ds(64 * half, 64)
        return rcopy(qfin.at[0, rows], qfin.at[1, rows], ss.at[25 + half], cr.at[5 + half], other)

    def query_half(half, u):
        for i in (2, 1, 3, 0):
            tile = dqt[half, :, pl.ds((i + 4 * u) * HD, HD)].T.astype(BF)
            for h in range(2):
                dqs[i + 4 * u, pl.ds(64 * half, 64), pl.ds(HD * h, HD)] = tile[64 * h : 64 * h + 64]
            if i:
                rx_copy(i, half, u).start()

    def presum(s):
        rs_copy(s).wait_recv()
        for d in (2, 1, 3):
            acc[s, d] = (dkv[s, c, d] + sib[s, d].astype(F32)).astype(BF)

    def stage_a(s):
        presum(s)
        ra_top(s).start()
        ra_bot(s).start()

    def stage_direct(s):
        presum(s)
        ro_copy(s).start()
        rb_up(s).start()
        rb_down(s).start()

    def stage_b(s):
        ra_top(s).wait_recv()
        acc[s, 1, top] = (acc[s, 1, top].astype(F32) + fa[s - 2].astype(F32)).astype(BF)
        rb_up(s).start()
        ra_bot(s).wait_recv()
        acc[s, 3, bot] = (acc[s, 3, bot].astype(F32) + fb[s - 2].astype(F32)).astype(BF)
        rb_down(s).start()

    def own_sum(s):
        rb_up(s).wait_recv()
        rb_down(s).wait_recv()
        return dkv[s, c, 0] + sib[s, 0].astype(F32) + ra[s].astype(F32) + rb[s].astype(F32)

    def direct_sum(s):
        t = own_sum(s)
        ro_copy(s).wait_recv()
        return t + rc[s].astype(F32)

    def to_owner(s, total):
        zb[s] = total.astype(BF)
        rz_copy(s).start()

    full_up(0).start()
    full_down(0).start()
    opp0.start()
    for s in (1, 2, 3):
        pz_copy(s).start()
    for n in (0, 2, 1, 3):
        x_copy(n, 0).start()
    for s in (1, 2, 3):
        z_copy(s).start()
    for half in range(2):
        zq_copy(half).start()
    for d in (1, 2, 3):
        m_copy(d).start()
    mz_copy.start()
    stage_full(1)
    full_up(0).wait_recv()
    full_down(0).wait_recv()
    opp0.wait_recv()
    sib_rest(0).start()
    x_copy(0, 0).wait_recv()
    x_copy(4, 0).start()
    x_copy(2, 0).wait_recv()
    x_copy(5, 0).start()
    stage_full(2)
    all_of(kp.at[0, rest], cr.at[0]).wait()
    for d in (1, 2, 3):
        ky_copy(d).start()
    zq_copy(0).wait_recv()
    x_copy(0, 1).start()
    stage_full(3)
    stage_half(1)
    zq_copy(1).wait_recv()
    for n in (2, 1, 3):
        x_copy(n, 1).start()
    all_of(sm.at[4], cr.at[10]).wait()
    for d in (1, 2, 3):
        m2_copy(d).start()
    stage_half(2)
    all_of(sm.at[rest], cr.at[2]).wait()
    prepare_rows(sm, rw, range(4))
    for n in (1, 3, 4, 5):
        x_copy(n, 0).wait_recv()
    stage_half(3)
    stage_sib(1)
    all_of(kp.at[rest], cr.at[1]).wait()

    def own_queries(s, carry):
        @pl.when(s == 1)
        def _():
            x_copy(0, 1).wait_recv()
            x_copy(4, 1).start()
            x_copy(2, 1).wait_recv()
            x_copy(5, 1).start()

        @pl.when(s > 0)
        def _():
            all_of(kv.at[1 - c, s], br.at[s]).wait()

        @pl.when(s == 0)
        def _():
            all_of(kv.at[1 - c, 0, rest], br.at[0]).wait()

        key_half(s, 0, 0, qx, rw, kv, kp, dkv, dqt)

        @pl.when(s < 2)
        def _():
            stage_sib(s + 2)

        key_half(s, 1, 0, qx, rw, kv, kp, dkv, dqt)
        return carry

    lax.fori_loop(0, 4, own_queries, 0)
    for half in range(2):
        query_half(half, 0)
    all_of(sm.at[pl.ds(5, 3)], cr.at[11]).wait()
    prepare_rows(sm, rw, range(4, 8))
    for n in (1, 3, 4, 5):
        x_copy(n, 1).wait_recv()

    def partner_queries(t, carry):
        s = 3 - t

        @pl.when(t >= 2)
        def _():
            stage_a(s + 2)

        key_half(s, 0, 1, qx, rw, kv, kp, dkv, dqt)

        @pl.when(t == 3)
        def _():
            query_half(0, 1)

        key_half(s, 1, 1, qx, rw, kv, kp, dkv, dqt)
        so[s] = dkv[s, 1 - c].astype(BF)
        rs_copy(s).start()
        return carry

    lax.fori_loop(0, 4, partner_queries, 0)
    query_half(1, 1)
    stage_direct(1)
    stage_b(3)
    stage_b(2)
    stage_direct(0)
    all_of(kv.at[c, rest, 0], ss.at[0]).wait()
    all_of(kp.at[0, rest], ss.at[1]).wait()
    all_of(kp.at[rest], ss.at[2]).wait()
    all_of(kv.at[c, :, 0], ss.at[3]).wait()
    all_of(kv.at[c, :, 0], ss.at[4]).wait()
    all_of(kv.at[c, rest, 2, top], ss.at[5]).wait()
    all_of(kv.at[c, rest, 2, bot], ss.at[6]).wait()
    opp0.wait_send()
    all_of(kv.at[c, rest, 0], ss.at[8]).wait()
    all_of(kv.at[c, :, rest], ss.at[9]).wait()
    for u in range(2):
        for n in range(6):
            x_copy(n, u).wait_send()
    all_of(qx.at[:, :, 4], ss.at[34]).wait()
    all_of(sm.at[rest], ss.at[16]).wait()
    all_of(sm.at[4], ss.at[35]).wait()
    all_of(sm.at[pl.ds(5, 3)], ss.at[36]).wait()
    all_of(qin.at[rest], cr.at[4]).wait()
    qsum = dqs[0].astype(F32)
    for d in (1, 2, 3):
        qsum = qsum + qin[d].astype(F32)
    to_owner(3, own_sum(3))
    to_owner(1, direct_sum(1))
    to_owner(2, own_sum(2))
    tot0[...] = direct_sum(0)
    for half in range(2):
        rows = pl.ds(64 * half, 64)
        all_of(qin.at[pl.ds(5, 3), rows], cr.at[12 + half]).wait()
        psum = dqs[4, rows].astype(F32)
        for d in (1, 2, 3):
            psum = psum + qin[4 + d, rows].astype(F32)
        qb[rows] = psum.astype(BF)
        rp_copy(half).start()
    all_of(zin.at[rest], cr.at[3]).wait()
    tot = tot0[...]
    for s in (1, 2, 3):
        tot = tot + zin[s].astype(F32)
    fin[0] = tot.astype(BF)
    sk = rcopy(fin.at[0], fin.at[1], ss.at[27], cr.at[7], other)
    sk.start()
    for half in range(2):
        rows = pl.ds(64 * half, 64)
        rp_copy(half).wait_recv()
        qfin[0, rows] = (qsum[64 * half : 64 * half + 64] + qp[rows].astype(F32)).astype(BF)
        share(half).start()
    all_of(sib, ss.at[17]).wait()
    all_of(fa, ss.at[18]).wait()
    all_of(fb, ss.at[19]).wait()
    all_of(ra, ss.at[20]).wait()
    all_of(rb, ss.at[21]).wait()
    all_of(rc, ss.at[22]).wait()
    all_of(zin.at[rest], ss.at[23]).wait()
    all_of(qin.at[rest], ss.at[24]).wait()
    all_of(qin.at[pl.ds(5, 3)], ss.at[37]).wait()
    all_of(qp, ss.at[38]).wait()
    low = c == 0
    sk.wait()
    gk_ref[...] = jnp.where(low, fin[0], fin[1])
    gv_ref[...] = jnp.where(low, fin[1], fin[0])
    for half in range(2):
        share(half).wait()
    gq_ref[:, 0:256] = jnp.where(low, qfin[0], qfin[1])
    gq_ref[:, 256:512] = jnp.where(low, qfin[1], qfin[0])


def hand_on(a_ref, b_ref, c_ref, ao_ref, bo_ref, co_ref):
    ao_ref[...] = a_ref[...]
    bo_ref[...] = b_ref[...]
    co_ref[...] = c_ref[...]


VM = pl.BlockSpec(memory_space=pltpu.VMEM)
DMA = pltpu.SemaphoreType.DMA


def per_device(queries, keys, values, output, grad_out, lse, positions):
    partial = pl.pallas_call(
        fused_kernel,
        out_shape=(
            jax.ShapeDtypeStruct((128, 512), BF),
            jax.ShapeDtypeStruct((128, 128), BF),
            jax.ShapeDtypeStruct((128, 128), BF),
        ),
        in_specs=[pl.BlockSpec(memory_space=pltpu.HBM)] * 7,
        out_specs=(VM,) * 3,
        scratch_shapes=[
            pltpu.VMEM((2, 2, 8, 128, 128), BF),
            pltpu.VMEM((8, 8, 128), F32),
            pltpu.VMEM((2, 4, 4, 128, 128), BF),
            pltpu.VMEM((4, 4, 1, 128), jnp.int32),
            pltpu.VMEM((8, 1024), F32),
            pltpu.VMEM((2, 128, 1024), F32),
            pltpu.VMEM((4, 2, 4, 128, 128), F32),
            pltpu.VMEM((4, 4, 128, 128), BF),
            pltpu.VMEM((4, 4, 128, 128), BF),
            pltpu.VMEM((4, 4, 128, 128), BF),
            pltpu.VMEM((2, 64, 128), BF),
            pltpu.VMEM((2, 64, 128), BF),
            pltpu.VMEM((4, 128, 128), BF),
            pltpu.VMEM((4, 128, 128), BF),
            pltpu.VMEM((2, 128, 128), BF),
            pltpu.VMEM((4, 128, 128), BF),
            pltpu.VMEM((4, 128, 128), BF),
            pltpu.VMEM((128, 128), F32),
            pltpu.VMEM((8, 128, 256), BF),
            pltpu.VMEM((8, 128, 256), BF),
            pltpu.VMEM((128, 256), BF),
            pltpu.VMEM((128, 256), BF),
            pltpu.VMEM((2, 128, 128), BF),
            pltpu.VMEM((2, 128, 256), BF),
            pltpu.VMEM((2, 128, 128), BF),
            pltpu.VMEM((4, 128), F32),
            pltpu.VMEM((1, 128), jnp.int32),
            DMA((39,)), DMA((4,)), DMA((4, 4)), DMA((4,)), DMA((2, 6)), DMA((16,)), DMA((4,)), DMA((4, 4)), DMA((7,)),
        ],
        compiler_params=pltpu.CompilerParams(
            collective_id=0, has_side_effects=True
        ),
        name="attention_grad",
    )(queries, keys, values, output, grad_out, lse, positions.reshape(1, 128))
    return pl.pallas_call(
        hand_on,
        out_shape=tuple(jax.ShapeDtypeStruct(a.shape, a.dtype) for a in partial),
        in_specs=[VM] * 3,
        out_specs=(VM,) * 3,
        name="hand_on",
    )(*partial)


def solution(mesh):
    placed = (
        P("blk", None),
        P("blk", None),
        P("blk", None),
        P("blk", None),
        P("blk", None),
        P(None, "blk"),
        P("blk"),
    )
    return jax.shard_map(
        per_device,
        mesh=mesh,
        in_specs=placed,
        out_specs=(P("blk", None), P("blk", None), P("blk", None)),
        check_vma=False,
    )
```

```python
import math

import jax
import jax.numpy as jnp
from jax import lax
from jax.experimental import pallas as pl
from jax.experimental.pallas import tpu as pltpu
from jax.sharding import PartitionSpec as P

MESH = pl.DeviceIdType.MESH
BF = jnp.bfloat16
F32 = jnp.float32
HD = 128
SCALE = HD ** (-0.5)
LOG2E = math.log2(math.e)
BIG = 1e30


def coords():
    b = lax.axis_index("blk")
    r = lax.axis_index("rep")
    x = b // 32
    y = b % 4
    z = (r // 2) * 8 + (b // 4) % 8
    return x, y, z, r % 2


def dev(x, y, z, c):
    xx = (x + 4) % 4
    yy = (y + 4) % 4
    zz = (z + 16) % 16
    return ((xx * 8 + zz % 8) * 4 + yy, (zz // 8) * 2 + c)


def entry_barrier(x, y, z, c):
    group = [dev(x, y, z, 1 - c)]
    for d in (1, 2, 3):
        group.append(dev(x + d, y, z, c))
        group.append(dev(x, y + d, z, c))
    for o in (1, 2, 3, -1, -2, -3):
        group.append(dev(x, y, z + o, c))
    barrier = pltpu.get_barrier_semaphore()
    for d in group:
        pl.semaphore_signal(barrier, inc=1, device_id=d, device_id_type=MESH)
    return barrier, len(group)


def rcopy(src, dst, ssem, rsem, device):
    return pltpu.make_async_remote_copy(
        src_ref=src, dst_ref=dst, send_sem=ssem, recv_sem=rsem, device_id=device, device_id_type=MESH
    )


def nt(a, b):
    return lax.dot_general(a, b, (((1,), (1,)), ((), ())), preferred_element_type=F32)


def nn(a, b):
    return lax.dot_general(a, b, (((1,), (0,)), ((), ())), preferred_element_type=F32)


def prepare_rows(sm_ref, rw, blocks):
    for i in blocks:
        rw[:, pl.ds(i * HD, HD)] = sm_ref[i]


def key_half(s, kh, u, qx, rw, kv_ref, kp_ref, dkv, dqt):
    rows = pl.ds(64 * kh, 64)
    kc = kv_ref[0, s, :, rows, :].reshape(256, HD)
    vc = kv_ref[1, s, :, rows, :].reshape(256, HD)
    kt = kc.T
    dk = jnp.zeros((256, HD), F32)
    dv = jnp.zeros((256, HD), F32)
    for half in ((0, 1) if kh == 0 else (1,)):
        for g in (2 * u, 2 * u + 1):
            ls = pl.ds(256 * g, 256)
            lse = rw[half : half + 1, ls]
            dlt = rw[2 + half : 3 + half, ls]
            if kh != half:
                le = jnp.broadcast_to(lse, (4, 256))
            else:
                qp = rw[4:5, ls].astype(jnp.int32) * 32768 + rw[5:6, ls].astype(jnp.int32)
                parts = []
                for yb in range(4):
                    kp = jnp.broadcast_to(kp_ref[yb, s][:, 0:1], (1, 256))
                    seen = kp <= qp if kh == 0 else kp >= qp
                    parts.append(jnp.where(seen, lse, BIG))
                le = jnp.concatenate(parts, axis=0)
            qg = qx[0, half, 2 * g : 2 * g + 2].reshape(256, HD)
            dg = qx[1, half, 2 * g : 2 * g + 2].reshape(256, HD)
            sc = nt(kc, qg).reshape(4, 64, 256)
            dp = nt(vc, dg)
            t = (sc * (SCALE * LOG2E) - le[:, None, :]).reshape(256, 256)
            if kh == half and g == 0:
                ri = lax.broadcasted_iota(jnp.int32, (64, HD), 0)
                li = lax.broadcasted_iota(jnp.int32, (64, HD), 1)
                own = jnp.where(ri <= li % 64 + 64 * s, t[:64, :HD], -BIG)
                t = jnp.concatenate([jnp.concatenate([own, t[:64, HD:]], axis=1), t[64:]], axis=0)
            p = jnp.exp2(t)
            ds = (p * (dp * SCALE - dlt)).astype(BF)
            dv = dv + nn(p.astype(BF), dg)
            dk = dk + nn(ds, qg)
            dqt[half, :, ls] += nn(kt, ds)
    if u:
        dk = dk + dkv[s, 0, :, rows, :].reshape(256, HD)
        dv = dv + dkv[s, 1, :, rows, :].reshape(256, HD)
    dkv[s, 0, :, rows, :] = dk.reshape(4, 64, HD)
    dkv[s, 1, :, rows, :] = dv.reshape(4, 64, HD)


def fused_kernel(
    q_ref, k_ref, v_ref, o_ref, do_ref, lse_ref, pos_ref,
    gq_ref, gk_ref, gv_ref,
    qx, sm, kv, kp, rw, dqt, dkv, so, sib, acc, fa, fb, ra, rb, rc, zb, zin, tot0, dqs, qin, qb, qp, fin, qfin,
    ov, lv, pv, ss, zr, yr, br, xr, cr, rbr, ryr, ir,
):
    x, y, z, c = coords()
    barrier, count = entry_barrier(x, y, z, c)
    other = dev(x, y, z, 1 - c)
    up, down = dev(x, y + 1, z, c), dev(x, y - 1, z, c)
    right, left = dev(x + 1, y, z, c), dev(x - 1, y, z, c)
    away = 2 * (z % 2) - 1
    partner = dev(x, y, z - away, c)
    top, bot = pl.ds(0, 64), pl.ds(64, 64)
    rest = pl.ds(1, 3)
    col = pl.multiple_of(c * 256, 256)

    def all_of(ref, sem):
        return pltpu.make_async_copy(ref, ref, sem)

    pltpu.make_async_copy(k_ref, kv.at[0, 0, 0], ir.at[0]).start()
    pltpu.make_async_copy(v_ref, kv.at[1, 0, 0], ir.at[1]).start()
    for n, ref, dst in ((2, do_ref, qx.at[1, :, 0]), (3, o_ref, ov), (4, q_ref, qx.at[0, :, 0])):
        for half in range(2):
            for h in range(2):
                pltpu.make_async_copy(
                    ref.at[pl.ds(64 * half, 64), pl.ds(col + HD * h, HD)], dst.at[half, pl.ds(64 * h, 64)], ir.at[n]
                ).start()
    pltpu.make_async_copy(lse_ref, lv, ir.at[5]).start()
    pltpu.make_async_copy(pos_ref, pv, ir.at[6]).start()
    all_of(qx.at[1, :, 0], ir.at[2]).wait()
    all_of(ov, ir.at[3]).wait()
    all_of(lv, ir.at[5]).wait()
    all_of(pv, ir.at[6]).wait()
    sel = lax.broadcasted_iota(jnp.int32, (1, HD), 1) < 64
    l0 = lv[pl.ds(2 * c, 1), :] * LOG2E
    l1 = lv[pl.ds(2 * c + 1, 1), :] * LOG2E
    rows = [jnp.where(sel, l0, pltpu.roll(l1, 64, 1)), jnp.where(sel, pltpu.roll(l0, 64, 1), l1)]
    for half in range(2):
        prod = qx[1, half, 0].astype(F32) * ov[half].astype(F32)
        total = jnp.sum(prod, axis=1, keepdims=True) * SCALE
        rows.append(jnp.broadcast_to(total, (HD, HD)).T[0:1, :])
    p = jnp.broadcast_to(pv[0:1, 0:1], (1, HD))
    rows.append((p // 32768).astype(F32))
    rows.append((p % 32768).astype(F32))
    rows.append(jnp.zeros((2, HD), F32))
    sm[0] = jnp.concatenate(rows, axis=0)
    kp[0, 0] = pv[...]
    dqt[...] = jnp.zeros_like(dqt)
    all_of(kv.at[0, 0, 0], ir.at[0]).wait()
    all_of(kv.at[1, 0, 0], ir.at[1]).wait()
    all_of(qx.at[0, :, 0], ir.at[4]).wait()
    pl.semaphore_wait(barrier, count)

    def z_copy(s):
        to = z + s * away if s % 2 else z - s * away
        return rcopy(kv.at[c, 0, 0], kv.at[c, s, 0], ss.at[0], zr.at[s], dev(x, y, to, c))

    def pz_copy(s):
        to = z + s * away if s % 2 else z - s * away
        return rcopy(kp.at[0, 0], kp.at[0, s], ss.at[1], cr.at[0], dev(x, y, to, c))

    def ky_copy(d):
        return rcopy(kp.at[0], kp.at[d], ss.at[2], cr.at[1], dev(x, y - d, z, c))

    def full_up(s):
        return rcopy(kv.at[c, s, 0], kv.at[c, s, 3], ss.at[3], yr.at[s, 0], up)

    def full_down(s):
        return rcopy(kv.at[c, s, 0], kv.at[c, s, 1], ss.at[4], yr.at[s, 1], down)

    def half_up(s):
        return rcopy(kv.at[c, s, 3, top], kv.at[c, s, 2, top], ss.at[5], yr.at[s, 2], up)

    def half_down(s):
        return rcopy(kv.at[c, s, 1, bot], kv.at[c, s, 2, bot], ss.at[6], yr.at[s, 3], down)

    opp0 = rcopy(kv.at[c, 0, 0], kv.at[c, 0, 2], ss.at[7], yr.at[0, 2], dev(x, y + 2, z, c))

    def sib_own(s):
        return rcopy(kv.at[c, s, 0], kv.at[c, s, 0], ss.at[8], br.at[s], other)

    def sib_rest(s):
        return rcopy(kv.at[c, s, rest], kv.at[c, s, rest], ss.at[9], br.at[s], other)

    def x_copy(n, u):
        src, dst, half, to = (
            (0, 3, 0, right), (0, 3, 1, right), (0, 1, 1, left), (0, 1, 0, left), (3, 2, 0, right), (1, 2, 1, left)
        )[n]
        return rcopy(
            qx.at[:, half, src + 4 * u], qx.at[:, half, dst + 4 * u], ss.at[10 + n + 18 * u], xr.at[u, n], to
        )

    def zq_copy(half):
        return rcopy(qx.at[:, half, 0], qx.at[:, half, 4], ss.at[34], cr.at[8 + half], partner)

    def m_copy(d):
        return rcopy(sm.at[0], sm.at[d], ss.at[16], cr.at[2], dev(x - d, y, z, c))

    mz_copy = rcopy(sm.at[0], sm.at[4], ss.at[35], cr.at[10], partner)

    def m2_copy(d):
        return rcopy(sm.at[4], sm.at[4 + d], ss.at[36], cr.at[11], dev(x - d, y, z, c))

    def stage_full(s):
        z_copy(s).wait_recv()
        full_up(s).start()
        full_down(s).start()
        sib_own(s).start()

    def stage_half(s):
        full_up(s).wait_recv()
        half_up(s).start()
        full_down(s).wait_recv()
        half_down(s).start()

    def stage_sib(s):
        half_up(s).wait_recv()
        half_down(s).wait_recv()
        sib_rest(s).start()

    def rs_copy(s):
        return rcopy(so.at[s], sib.at[s], ss.at[17], rbr.at[s], other)

    def ra_top(s):
        return rcopy(acc.at[s, 2, top], fa.at[s - 2], ss.at[18], ryr.at[s, 0], up)

    def ra_bot(s):
        return rcopy(acc.at[s, 2, bot], fb.at[s - 2], ss.at[19], ryr.at[s, 1], down)

    def rb_up(s):
        return rcopy(acc.at[s, 1], ra.at[s], ss.at[20], ryr.at[s, 2], up)

    def rb_down(s):
        return rcopy(acc.at[s, 3], rb.at[s], ss.at[21], ryr.at[s, 3], down)

    def ro_copy(s):
        return rcopy(acc.at[s, 2], rc.at[s], ss.at[22], ryr.at[s, 0], dev(x, y + 2, z, c))

    def rz_copy(s):
        return rcopy(zb.at[s], zin.at[s], ss.at[23], cr.at[3], dev(x, y, z + s * away, c))

    def rx_copy(d, half, u):
        rows = pl.ds(64 * half, 64)
        got = cr.at[12 + half] if u else cr.at[4]
        return rcopy(
            dqs.at[d + 4 * u, rows], qin.at[d + 4 * u, rows], ss.at[37 if u else 24], got, dev(x + d, y, z, c)
        )

    def rp_copy(half):
        rows = pl.ds(64 * half, 64)
        return rcopy(qb.at[rows], qp.at[rows], ss.at[38], cr.at[14 + half], partner)

    def share(half):
        rows = pl.ds(64 * half, 64)
        return rcopy(qfin.at[0, rows], qfin.at[1, rows], ss.at[25 + half], cr.at[5 + half], other)

    def query_half(half, u):
        for i in (2, 1, 3, 0):
            tile = dqt[half, :, pl.ds((i + 4 * u) * HD, HD)].T.astype(BF)
            for h in range(2):
                dqs[i + 4 * u, pl.ds(64 * half, 64), pl.ds(HD * h, HD)] = tile[64 * h : 64 * h + 64]
            if i:
                rx_copy(i, half, u).start()

    def presum(s):
        rs_copy(s).wait_recv()
        for d in (2, 1, 3):
            acc[s, d] = (dkv[s, c, d] + sib[s, d].astype(F32)).astype(BF)

    def stage_a(s):
        presum(s)
        ra_top(s).start()
        ra_bot(s).start()

    def stage_direct(s):
        presum(s)
        ro_copy(s).start()
        rb_up(s).start()
        rb_down(s).start()

    def stage_b(s):
        ra_top(s).wait_recv()
        acc[s, 1, top] = (acc[s, 1, top].astype(F32) + fa[s - 2].astype(F32)).astype(BF)
        rb_up(s).start()
        ra_bot(s).wait_recv()
        acc[s, 3, bot] = (acc[s, 3, bot].astype(F32) + fb[s - 2].astype(F32)).astype(BF)
        rb_down(s).start()

    def own_sum(s):
        rb_up(s).wait_recv()
        rb_down(s).wait_recv()
        return dkv[s, c, 0] + sib[s, 0].astype(F32) + ra[s].astype(F32) + rb[s].astype(F32)

    def direct_sum(s):
        t = own_sum(s)
        ro_copy(s).wait_recv()
        return t + rc[s].astype(F32)

    def to_owner(s, total):
        zb[s] = total.astype(BF)
        rz_copy(s).start()

    full_up(0).start()
    full_down(0).start()
    opp0.start()
    for s in (1, 2, 3):
        pz_copy(s).start()
    for n in (0, 2, 1, 3):
        x_copy(n, 0).start()
    for s in (1, 2, 3):
        z_copy(s).start()
    for half in range(2):
        zq_copy(half).start()
    for d in (1, 2, 3):
        m_copy(d).start()
    mz_copy.start()
    stage_full(1)
    full_up(0).wait_recv()
    full_down(0).wait_recv()
    opp0.wait_recv()
    sib_rest(0).start()
    x_copy(0, 0).wait_recv()
    x_copy(4, 0).start()
    x_copy(2, 0).wait_recv()
    x_copy(5, 0).start()
    stage_full(2)
    all_of(kp.at[0, rest], cr.at[0]).wait()
    for d in (1, 2, 3):
        ky_copy(d).start()
    zq_copy(0).wait_recv()
    x_copy(0, 1).start()
    stage_full(3)
    stage_half(1)
    zq_copy(1).wait_recv()
    for n in (2, 1, 3):
        x_copy(n, 1).start()
    all_of(sm.at[4], cr.at[10]).wait()
    for d in (1, 2, 3):
        m2_copy(d).start()
    stage_half(2)
    all_of(sm.at[rest], cr.at[2]).wait()
    prepare_rows(sm, rw, range(4))
    for n in (1, 3, 4, 5):
        x_copy(n, 0).wait_recv()
    stage_half(3)
    stage_sib(1)
    all_of(kp.at[rest], cr.at[1]).wait()

    def own_queries(s, carry):
        @pl.when(s == 1)
        def _():
            x_copy(0, 1).wait_recv()
            x_copy(4, 1).start()
            x_copy(2, 1).wait_recv()
            x_copy(5, 1).start()

        @pl.when(s > 0)
        def _():
            all_of(kv.at[1 - c, s], br.at[s]).wait()

        @pl.when(s == 0)
        def _():
            all_of(kv.at[1 - c, 0, rest], br.at[0]).wait()

        key_half(s, 0, 0, qx, rw, kv, kp, dkv, dqt)

        @pl.when(s < 2)
        def _():
            stage_sib(s + 2)

        key_half(s, 1, 0, qx, rw, kv, kp, dkv, dqt)
        return carry

    lax.fori_loop(0, 4, own_queries, 0)
    for half in range(2):
        query_half(half, 0)
    all_of(sm.at[pl.ds(5, 3)], cr.at[11]).wait()
    prepare_rows(sm, rw, range(4, 8))
    for n in (1, 3, 4, 5):
        x_copy(n, 1).wait_recv()

    def partner_queries(t, carry):
        s = 3 - t

        @pl.when(t >= 2)
        def _():
            stage_a(s + 2)

        key_half(s, 0, 1, qx, rw, kv, kp, dkv, dqt)

        @pl.when(t == 3)
        def _():
            query_half(0, 1)

        key_half(s, 1, 1, qx, rw, kv, kp, dkv, dqt)
        so[s] = dkv[s, 1 - c].astype(BF)
        rs_copy(s).start()
        return carry

    lax.fori_loop(0, 4, partner_queries, 0)
    query_half(1, 1)
    stage_direct(1)
    stage_b(3)
    stage_b(2)
    stage_direct(0)
    all_of(kv.at[c, rest, 0], ss.at[0]).wait()
    all_of(kp.at[0, rest], ss.at[1]).wait()
    all_of(kp.at[rest], ss.at[2]).wait()
    all_of(kv.at[c, :, 0], ss.at[3]).wait()
    all_of(kv.at[c, :, 0], ss.at[4]).wait()
    all_of(kv.at[c, rest, 2, top], ss.at[5]).wait()
    all_of(kv.at[c, rest, 2, bot], ss.at[6]).wait()
    opp0.wait_send()
    all_of(kv.at[c, rest, 0], ss.at[8]).wait()
    all_of(kv.at[c, :, rest], ss.at[9]).wait()
    for u in range(2):
        for n in range(6):
            x_copy(n, u).wait_send()
    all_of(qx.at[:, :, 4], ss.at[34]).wait()
    all_of(sm.at[rest], ss.at[16]).wait()
    all_of(sm.at[4], ss.at[35]).wait()
    all_of(sm.at[pl.ds(5, 3)], ss.at[36]).wait()
    all_of(qin.at[rest], cr.at[4]).wait()
    qsum = dqs[0].astype(F32)
    for d in (1, 2, 3):
        qsum = qsum + qin[d].astype(F32)
    to_owner(3, own_sum(3))
    to_owner(1, direct_sum(1))
    to_owner(2, own_sum(2))
    tot0[...] = direct_sum(0)
    for half in range(2):
        rows = pl.ds(64 * half, 64)
        all_of(qin.at[pl.ds(5, 3), rows], cr.at[12 + half]).wait()
        psum = dqs[4, rows].astype(F32)
        for d in (1, 2, 3):
            psum = psum + qin[4 + d, rows].astype(F32)
        qb[rows] = psum.astype(BF)
        rp_copy(half).start()
    all_of(zin.at[rest], cr.at[3]).wait()
    tot = tot0[...]
    for s in (1, 2, 3):
        tot = tot + zin[s].astype(F32)
    fin[0] = tot.astype(BF)
    sk = rcopy(fin.at[0], fin.at[1], ss.at[27], cr.at[7], other)
    sk.start()
    for half in range(2):
        rows = pl.ds(64 * half, 64)
        rp_copy(half).wait_recv()
        qfin[0, rows] = (qsum[64 * half : 64 * half + 64] + qp[rows].astype(F32)).astype(BF)
        share(half).start()
    all_of(sib, ss.at[17]).wait()
    all_of(fa, ss.at[18]).wait()
    all_of(fb, ss.at[19]).wait()
    all_of(ra, ss.at[20]).wait()
    all_of(rb, ss.at[21]).wait()
    all_of(rc, ss.at[22]).wait()
    all_of(zin.at[rest], ss.at[23]).wait()
    all_of(qin.at[rest], ss.at[24]).wait()
    all_of(qin.at[pl.ds(5, 3)], ss.at[37]).wait()
    all_of(qp, ss.at[38]).wait()
    low = c == 0
    sk.wait()
    gk_ref[...] = jnp.where(low, fin[0], fin[1])
    gv_ref[...] = jnp.where(low, fin[1], fin[0])
    for half in range(2):
        share(half).wait()
    gq_ref[:, 0:256] = jnp.where(low, qfin[0], qfin[1])
    gq_ref[:, 256:512] = jnp.where(low, qfin[1], qfin[0])


def hand_on(a_ref, b_ref, c_ref, ao_ref, bo_ref, co_ref):
    ao_ref[...] = a_ref[...]
    bo_ref[...] = b_ref[...]
    co_ref[...] = c_ref[...]


VM = pl.BlockSpec(memory_space=pltpu.VMEM)
DMA = pltpu.SemaphoreType.DMA


def per_device(queries, keys, values, output, grad_out, lse, positions):
    partial = pl.pallas_call(
        fused_kernel,
        out_shape=(
            jax.ShapeDtypeStruct((128, 512), BF),
            jax.ShapeDtypeStruct((128, 128), BF),
            jax.ShapeDtypeStruct((128, 128), BF),
        ),
        in_specs=[pl.BlockSpec(memory_space=pltpu.HBM)] * 7,
        out_specs=(VM,) * 3,
        scratch_shapes=[
            pltpu.VMEM((2, 2, 8, 128, 128), BF),
            pltpu.VMEM((8, 8, 128), F32),
            pltpu.VMEM((2, 4, 4, 128, 128), BF),
            pltpu.VMEM((4, 4, 1, 128), jnp.int32),
            pltpu.VMEM((8, 1024), F32),
            pltpu.VMEM((2, 128, 1024), F32),
            pltpu.VMEM((4, 2, 4, 128, 128), F32),
            pltpu.VMEM((4, 4, 128, 128), BF),
            pltpu.VMEM((4, 4, 128, 128), BF),
            pltpu.VMEM((4, 4, 128, 128), BF),
            pltpu.VMEM((2, 64, 128), BF),
            pltpu.VMEM((2, 64, 128), BF),
            pltpu.VMEM((4, 128, 128), BF),
            pltpu.VMEM((4, 128, 128), BF),
            pltpu.VMEM((2, 128, 128), BF),
            pltpu.VMEM((4, 128, 128), BF),
            pltpu.VMEM((4, 128, 128), BF),
            pltpu.VMEM((128, 128), F32),
            pltpu.VMEM((8, 128, 256), BF),
            pltpu.VMEM((8, 128, 256), BF),
            pltpu.VMEM((128, 256), BF),
            pltpu.VMEM((128, 256), BF),
            pltpu.VMEM((2, 128, 128), BF),
            pltpu.VMEM((2, 128, 256), BF),
            pltpu.VMEM((2, 128, 128), BF),
            pltpu.VMEM((4, 128), F32),
            pltpu.VMEM((1, 128), jnp.int32),
            DMA((39,)), DMA((4,)), DMA((4, 4)), DMA((4,)), DMA((2, 6)), DMA((16,)), DMA((4,)), DMA((4, 4)), DMA((7,)),
        ],
        compiler_params=pltpu.CompilerParams(
            collective_id=0, has_side_effects=True, vmem_limit_bytes=24 * 2**20
        ),
        name="attention_grad",
    )(
        *(
            pltpu.with_memory_space_constraint(a, pltpu.HBM)
            for a in (queries, keys, values, output, grad_out, lse, positions.reshape(1, 128))
        )
    )
    return pl.pallas_call(
        hand_on,
        out_shape=tuple(jax.ShapeDtypeStruct(a.shape, a.dtype) for a in partial),
        in_specs=[VM] * 3,
        out_specs=(VM,) * 3,
        compiler_params=pltpu.CompilerParams(vmem_limit_bytes=4 * 2**20),
        name="hand_on",
    )(*partial)


def solution(mesh):
    placed = (
        P("blk", None),
        P("blk", None),
        P("blk", None),
        P("blk", None),
        P("blk", None),
        P(None, "blk"),
        P("blk"),
    )
    return jax.shard_map(
        per_device,
        mesh=mesh,
        in_specs=placed,
        out_specs=(P("blk", None), P("blk", None), P("blk", None)),
        check_vma=False,
    )
```

```python
import math

import jax
import jax.numpy as jnp
from jax import lax
from jax.experimental import pallas as pl
from jax.experimental.pallas import tpu as pltpu
from jax.sharding import PartitionSpec as P

MESH = pl.DeviceIdType.MESH
BF = jnp.bfloat16
F32 = jnp.float32
HD = 128
SCALE = HD ** (-0.5)
LOG2E = math.log2(math.e)
BIG = 1e30


def coords():
    b = lax.axis_index("blk")
    r = lax.axis_index("rep")
    x = b // 32
    y = b % 4
    z = (r // 2) * 8 + (b // 4) % 8
    return x, y, z, r % 2


def dev(x, y, z, c):
    xx = (x + 4) % 4
    yy = (y + 4) % 4
    zz = (z + 16) % 16
    return ((xx * 8 + zz % 8) * 4 + yy, (zz // 8) * 2 + c)


def entry_barrier(x, y, z, c):
    group = [dev(x, y, z, 1 - c)]
    for d in (1, 2, 3):
        group.append(dev(x + d, y, z, c))
        group.append(dev(x, y + d, z, c))
    for o in (1, 2, 3, -1, -2, -3):
        group.append(dev(x, y, z + o, c))
    barrier = pltpu.get_barrier_semaphore()
    for d in group:
        pl.semaphore_signal(barrier, inc=1, device_id=d, device_id_type=MESH)
    return barrier, len(group)


def rcopy(src, dst, ssem, rsem, device):
    return pltpu.make_async_remote_copy(
        src_ref=src, dst_ref=dst, send_sem=ssem, recv_sem=rsem, device_id=device, device_id_type=MESH
    )


def nt(a, b):
    return lax.dot_general(a, b, (((1,), (1,)), ((), ())), preferred_element_type=F32)


def nn(a, b):
    return lax.dot_general(a, b, (((1,), (0,)), ((), ())), preferred_element_type=F32)


def prepare_rows(sm_ref, rw, blocks):
    for i in blocks:
        rw[:, pl.ds(i * HD, HD)] = sm_ref[i]


def key_half(s, kh, u, qx, rw, kv_ref, kp_ref, dkv, dqt):
    rows = pl.ds(64 * kh, 64)
    kc = kv_ref[0, s, :, rows, :].reshape(256, HD)
    vc = kv_ref[1, s, :, rows, :].reshape(256, HD)
    kt = kc.T
    dk = jnp.zeros((256, HD), F32)
    dv = jnp.zeros((256, HD), F32)
    for half in ((0, 1) if kh == 0 else (1,)):
        for g in (2 * u, 2 * u + 1):
            ls = pl.ds(256 * g, 256)
            lse = rw[half : half + 1, ls]
            dlt = rw[2 + half : 3 + half, ls]
            if kh != half:
                le = jnp.broadcast_to(lse, (4, 256))
            else:
                qp = rw[4:5, ls].astype(jnp.int32) * 32768 + rw[5:6, ls].astype(jnp.int32)
                parts = []
                for yb in range(4):
                    kp = jnp.broadcast_to(kp_ref[yb, s][:, 0:1], (1, 256))
                    seen = kp <= qp if kh == 0 else kp >= qp
                    parts.append(jnp.where(seen, lse, BIG))
                le = jnp.concatenate(parts, axis=0)
            qg = qx[0, half, 2 * g : 2 * g + 2].reshape(256, HD)
            dg = qx[1, half, 2 * g : 2 * g + 2].reshape(256, HD)
            sc = nt(kc, qg).reshape(4, 64, 256)
            dp = nt(vc, dg)
            t = (sc * (SCALE * LOG2E) - le[:, None, :]).reshape(256, 256)
            if kh == half and g == 0:
                ri = lax.broadcasted_iota(jnp.int32, (64, HD), 0)
                li = lax.broadcasted_iota(jnp.int32, (64, HD), 1)
                own = jnp.where(ri <= li % 64 + 64 * s, t[:64, :HD], -BIG)
                t = jnp.concatenate([jnp.concatenate([own, t[:64, HD:]], axis=1), t[64:]], axis=0)
            p = jnp.exp2(t)
            ds = (p * (dp * SCALE - dlt)).astype(BF)
            dv = dv + nn(p.astype(BF), dg)
            dk = dk + nn(ds, qg)
            dqt[half, :, ls] += nn(kt, ds)
    if u:
        dk = dk + dkv[s, 0, :, rows, :].reshape(256, HD)
        dv = dv + dkv[s, 1, :, rows, :].reshape(256, HD)
    dkv[s, 0, :, rows, :] = dk.reshape(4, 64, HD)
    dkv[s, 1, :, rows, :] = dv.reshape(4, 64, HD)


def fused_kernel(
    q_ref, k_ref, v_ref, o_ref, do_ref, lse_ref, pos_ref,
    gq_ref, gk_ref, gv_ref,
    qx, sm, kv, kp, rw, dqt, dkv, so, sib, acc, fa, fb, ra, rb, rc, zb, zin, tot0, dqs, qin, qb, qp, fin, qfin,
    ov, lv, pv, ss, zr, yr, br, xr, cr, rbr, ryr, ir,
):
    x, y, z, c = coords()
    barrier, count = entry_barrier(x, y, z, c)
    other = dev(x, y, z, 1 - c)
    up, down = dev(x, y + 1, z, c), dev(x, y - 1, z, c)
    right, left = dev(x + 1, y, z, c), dev(x - 1, y, z, c)
    away = 2 * (z % 2) - 1
    partner = dev(x, y, z - away, c)
    top, bot = pl.ds(0, 64), pl.ds(64, 64)
    rest = pl.ds(1, 3)
    col = pl.multiple_of(c * 256, 256)

    def all_of(ref, sem):
        return pltpu.make_async_copy(ref, ref, sem)

    pltpu.make_async_copy(k_ref, kv.at[0, 0, 0], ir.at[0]).start()
    pltpu.make_async_copy(v_ref, kv.at[1, 0, 0], ir.at[1]).start()
    for n, ref, dst in ((2, do_ref, qx.at[1, :, 0]), (3, o_ref, ov), (4, q_ref, qx.at[0, :, 0])):
        for half in range(2):
            for h in range(2):
                pltpu.make_async_copy(
                    ref.at[pl.ds(64 * half, 64), pl.ds(col + HD * h, HD)], dst.at[half, pl.ds(64 * h, 64)], ir.at[n]
                ).start()
    pltpu.make_async_copy(lse_ref, lv, ir.at[5]).start()
    pltpu.make_async_copy(pos_ref, pv, ir.at[6]).start()
    all_of(qx.at[1, :, 0], ir.at[2]).wait()
    all_of(ov, ir.at[3]).wait()
    all_of(lv, ir.at[5]).wait()
    all_of(pv, ir.at[6]).wait()
    sel = lax.broadcasted_iota(jnp.int32, (1, HD), 1) < 64
    l0 = lv[pl.ds(2 * c, 1), :] * LOG2E
    l1 = lv[pl.ds(2 * c + 1, 1), :] * LOG2E
    rows = [jnp.where(sel, l0, pltpu.roll(l1, 64, 1)), jnp.where(sel, pltpu.roll(l0, 64, 1), l1)]
    for half in range(2):
        prod = qx[1, half, 0].astype(F32) * ov[half].astype(F32)
        total = jnp.sum(prod, axis=1, keepdims=True) * SCALE
        rows.append(jnp.broadcast_to(total, (HD, HD)).T[0:1, :])
    p = jnp.broadcast_to(pv[0:1, 0:1], (1, HD))
    rows.append((p // 32768).astype(F32))
    rows.append((p % 32768).astype(F32))
    rows.append(jnp.zeros((2, HD), F32))
    sm[0] = jnp.concatenate(rows, axis=0)
    kp[0, 0] = pv[...]
    dqt[...] = jnp.zeros_like(dqt)
    all_of(kv.at[0, 0, 0], ir.at[0]).wait()
    all_of(kv.at[1, 0, 0], ir.at[1]).wait()
    all_of(qx.at[0, :, 0], ir.at[4]).wait()
    pl.semaphore_wait(barrier, count)

    def z_copy(s):
        to = z + s * away if s % 2 else z - s * away
        return rcopy(kv.at[c, 0, 0], kv.at[c, s, 0], ss.at[0], zr.at[s], dev(x, y, to, c))

    def pz_copy(s):
        to = z + s * away if s % 2 else z - s * away
        return rcopy(kp.at[0, 0], kp.at[0, s], ss.at[1], cr.at[0], dev(x, y, to, c))

    def ky_copy(d):
        return rcopy(kp.at[0], kp.at[d], ss.at[2], cr.at[1], dev(x, y - d, z, c))

    def full_up(s):
        return rcopy(kv.at[c, s, 0], kv.at[c, s, 3], ss.at[3], yr.at[s, 0], up)

    def full_down(s):
        return rcopy(kv.at[c, s, 0], kv.at[c, s, 1], ss.at[4], yr.at[s, 1], down)

    def half_up(s):
        return rcopy(kv.at[c, s, 3, top], kv.at[c, s, 2, top], ss.at[5], yr.at[s, 2], up)

    def half_down(s):
        return rcopy(kv.at[c, s, 1, bot], kv.at[c, s, 2, bot], ss.at[6], yr.at[s, 3], down)

    opp0 = rcopy(kv.at[c, 0, 0], kv.at[c, 0, 2], ss.at[7], yr.at[0, 2], dev(x, y + 2, z, c))

    def sib_own(s):
        return rcopy(kv.at[c, s, 0], kv.at[c, s, 0], ss.at[8], br.at[s], other)

    def sib_rest(s):
        return rcopy(kv.at[c, s, rest], kv.at[c, s, rest], ss.at[9], br.at[s], other)

    def x_copy(n, u):
        src, dst, half, to = (
            (0, 3, 0, right), (0, 3, 1, right), (0, 1, 1, left), (0, 1, 0, left), (3, 2, 0, right), (1, 2, 1, left)
        )[n]
        return rcopy(
            qx.at[:, half, src + 4 * u], qx.at[:, half, dst + 4 * u], ss.at[10 + u], xr.at[u, n], to
        )

    def zq_copy(half):
        return rcopy(qx.at[:, half, 0], qx.at[:, half, 4], ss.at[12], cr.at[8 + half], partner)

    def m_copy(d):
        return rcopy(sm.at[0], sm.at[d], ss.at[16], cr.at[2], dev(x - d, y, z, c))

    mz_copy = rcopy(sm.at[0], sm.at[4], ss.at[13], cr.at[10], partner)

    def m2_copy(d):
        return rcopy(sm.at[4], sm.at[4 + d], ss.at[14], cr.at[11], dev(x - d, y, z, c))

    def stage_full(s):
        z_copy(s).wait_recv()
        full_up(s).start()
        full_down(s).start()
        sib_own(s).start()

    def stage_half(s):
        full_up(s).wait_recv()
        half_up(s).start()
        full_down(s).wait_recv()
        half_down(s).start()

    def stage_sib(s):
        half_up(s).wait_recv()
        half_down(s).wait_recv()
        sib_rest(s).start()

    def rs_copy(s):
        return rcopy(so.at[s], sib.at[s], ss.at[17], rbr.at[s], other)

    def ra_top(s):
        return rcopy(acc.at[s, 2, top], fa.at[s - 2], ss.at[18], ryr.at[s, 0], up)

    def ra_bot(s):
        return rcopy(acc.at[s, 2, bot], fb.at[s - 2], ss.at[19], ryr.at[s, 1], down)

    def rb_up(s):
        return rcopy(acc.at[s, 1], ra.at[s], ss.at[20], ryr.at[s, 2], up)

    def rb_down(s):
        return rcopy(acc.at[s, 3], rb.at[s], ss.at[21], ryr.at[s, 3], down)

    def ro_copy(s):
        return rcopy(acc.at[s, 2], rc.at[s], ss.at[22], ryr.at[s, 0], dev(x, y + 2, z, c))

    def rz_copy(s):
        return rcopy(zb.at[s], zin.at[s], ss.at[23], cr.at[3], dev(x, y, z + s * away, c))

    def rx_copy(d, half, u):
        rows = pl.ds(64 * half, 64)
        got = cr.at[12 + half] if u else cr.at[4]
        return rcopy(
            dqs.at[d + 4 * u, rows], qin.at[d + 4 * u, rows], ss.at[15 if u else 24], got, dev(x + d, y, z, c)
        )

    def rp_copy(half):
        rows = pl.ds(64 * half, 64)
        return rcopy(qb.at[rows], qp.at[rows], ss.at[28], cr.at[14 + half], partner)

    def share(half):
        rows = pl.ds(64 * half, 64)
        return rcopy(qfin.at[0, rows], qfin.at[1, rows], ss.at[25 + half], cr.at[5 + half], other)

    def query_half(half, u):
        for i in (2, 1, 3, 0):
            tile = dqt[half, :, pl.ds((i + 4 * u) * HD, HD)].T.astype(BF)
            for h in range(2):
                dqs[i + 4 * u, pl.ds(64 * half, 64), pl.ds(HD * h, HD)] = tile[64 * h : 64 * h + 64]
            if i:
                rx_copy(i, half, u).start()

    def presum(s):
        rs_copy(s).wait_recv()
        for d in (2, 1, 3):
            acc[s, d] = (dkv[s, c, d] + sib[s, d].astype(F32)).astype(BF)

    def stage_a(s):
        presum(s)
        ra_top(s).start()
        ra_bot(s).start()

    def stage_direct(s):
        presum(s)
        ro_copy(s).start()
        rb_up(s).start()
        rb_down(s).start()

    def stage_b(s):
        ra_top(s).wait_recv()
        acc[s, 1, top] = (acc[s, 1, top].astype(F32) + fa[s - 2].astype(F32)).astype(BF)
        rb_up(s).start()
        ra_bot(s).wait_recv()
        acc[s, 3, bot] = (acc[s, 3, bot].astype(F32) + fb[s - 2].astype(F32)).astype(BF)
        rb_down(s).start()

    def own_sum(s):
        rb_up(s).wait_recv()
        rb_down(s).wait_recv()
        return dkv[s, c, 0] + sib[s, 0].astype(F32) + ra[s].astype(F32) + rb[s].astype(F32)

    def direct_sum(s):
        t = own_sum(s)
        ro_copy(s).wait_recv()
        return t + rc[s].astype(F32)

    def to_owner(s, total):
        zb[s] = total.astype(BF)
        rz_copy(s).start()

    full_up(0).start()
    full_down(0).start()
    opp0.start()
    for s in (1, 2, 3):
        pz_copy(s).start()
    for n in (0, 2, 1, 3):
        x_copy(n, 0).start()
    for s in (1, 2, 3):
        z_copy(s).start()
    for half in range(2):
        zq_copy(half).start()
    for d in (1, 2, 3):
        m_copy(d).start()
    mz_copy.start()
    stage_full(1)
    full_up(0).wait_recv()
    full_down(0).wait_recv()
    opp0.wait_recv()
    sib_rest(0).start()
    x_copy(0, 0).wait_recv()
    x_copy(4, 0).start()
    x_copy(2, 0).wait_recv()
    x_copy(5, 0).start()
    stage_full(2)
    all_of(kp.at[0, rest], cr.at[0]).wait()
    for d in (1, 2, 3):
        ky_copy(d).start()
    zq_copy(0).wait_recv()
    x_copy(0, 1).start()
    stage_full(3)
    stage_half(1)
    zq_copy(1).wait_recv()
    for n in (2, 1, 3):
        x_copy(n, 1).start()
    all_of(sm.at[4], cr.at[10]).wait()
    for d in (1, 2, 3):
        m2_copy(d).start()
    stage_half(2)
    all_of(sm.at[rest], cr.at[2]).wait()
    prepare_rows(sm, rw, range(4))
    for n in (1, 3, 4, 5):
        x_copy(n, 0).wait_recv()
    stage_half(3)
    stage_sib(1)
    all_of(kp.at[rest], cr.at[1]).wait()

    def own_queries(s, carry):
        @pl.when(s == 1)
        def _():
            x_copy(0, 1).wait_recv()
            x_copy(4, 1).start()
            x_copy(2, 1).wait_recv()
            x_copy(5, 1).start()

        @pl.when(s > 0)
        def _():
            all_of(kv.at[1 - c, s], br.at[s]).wait()

        @pl.when(s == 0)
        def _():
            all_of(kv.at[1 - c, 0, rest], br.at[0]).wait()

        key_half(s, 0, 0, qx, rw, kv, kp, dkv, dqt)

        @pl.when(s < 2)
        def _():
            stage_sib(s + 2)

        key_half(s, 1, 0, qx, rw, kv, kp, dkv, dqt)
        return carry

    lax.fori_loop(0, 4, own_queries, 0)
    for half in range(2):
        query_half(half, 0)
    all_of(sm.at[pl.ds(5, 3)], cr.at[11]).wait()
    prepare_rows(sm, rw, range(4, 8))
    for n in (1, 3, 4, 5):
        x_copy(n, 1).wait_recv()

    def partner_queries(t, carry):
        s = 3 - t

        @pl.when(t >= 2)
        def _():
            stage_a(s + 2)

        key_half(s, 0, 1, qx, rw, kv, kp, dkv, dqt)

        @pl.when(t == 3)
        def _():
            query_half(0, 1)

        key_half(s, 1, 1, qx, rw, kv, kp, dkv, dqt)
        so[s] = dkv[s, 1 - c].astype(BF)
        rs_copy(s).start()
        return carry

    lax.fori_loop(0, 4, partner_queries, 0)
    query_half(1, 1)
    stage_direct(1)
    stage_b(3)
    stage_b(2)
    stage_direct(0)
    all_of(kv.at[c, rest, 0], ss.at[0]).wait()
    all_of(kp.at[0, rest], ss.at[1]).wait()
    all_of(kp.at[rest], ss.at[2]).wait()
    all_of(kv.at[c, :, 0], ss.at[3]).wait()
    all_of(kv.at[c, :, 0], ss.at[4]).wait()
    all_of(kv.at[c, rest, 2, top], ss.at[5]).wait()
    all_of(kv.at[c, rest, 2, bot], ss.at[6]).wait()
    opp0.wait_send()
    all_of(kv.at[c, rest, 0], ss.at[8]).wait()
    all_of(kv.at[c, :, rest], ss.at[9]).wait()
    for u in range(2):
        all_of(qx.at[:, :, pl.ds(1 + 4 * u, 3)], ss.at[10 + u]).wait()
    all_of(qx.at[:, :, 4], ss.at[12]).wait()
    all_of(sm.at[rest], ss.at[16]).wait()
    all_of(sm.at[4], ss.at[13]).wait()
    all_of(sm.at[pl.ds(5, 3)], ss.at[14]).wait()
    all_of(qin.at[rest], cr.at[4]).wait()
    qsum = dqs[0].astype(F32)
    for d in (1, 2, 3):
        qsum = qsum + qin[d].astype(F32)

    def to_partner(half):
        rows = pl.ds(64 * half, 64)
        all_of(qin.at[pl.ds(5, 3), rows], cr.at[12 + half]).wait()
        psum = dqs[4, rows].astype(F32)
        for d in (1, 2, 3):
            psum = psum + qin[4 + d, rows].astype(F32)
        qb[rows] = psum.astype(BF)
        rp_copy(half).start()

    to_owner(3, own_sum(3))
    to_owner(1, direct_sum(1))
    to_partner(0)
    to_owner(2, own_sum(2))
    tot0[...] = direct_sum(0)
    to_partner(1)
    all_of(zin.at[rest], cr.at[3]).wait()
    tot = tot0[...]
    for s in (1, 2, 3):
        tot = tot + zin[s].astype(F32)
    fin[0] = tot.astype(BF)
    sk = rcopy(fin.at[0], fin.at[1], ss.at[27], cr.at[7], other)
    sk.start()
    for half in range(2):
        rows = pl.ds(64 * half, 64)
        rp_copy(half).wait_recv()
        qfin[0, rows] = (qsum[64 * half : 64 * half + 64] + qp[rows].astype(F32)).astype(BF)
        share(half).start()
    all_of(sib, ss.at[17]).wait()
    all_of(fa, ss.at[18]).wait()
    all_of(fb, ss.at[19]).wait()
    all_of(ra, ss.at[20]).wait()
    all_of(rb, ss.at[21]).wait()
    all_of(rc, ss.at[22]).wait()
    all_of(zin.at[rest], ss.at[23]).wait()
    all_of(qin.at[rest], ss.at[24]).wait()
    all_of(qin.at[pl.ds(5, 3)], ss.at[15]).wait()
    all_of(qp, ss.at[28]).wait()
    low = c == 0
    sk.wait()
    gk_ref[...] = jnp.where(low, fin[0], fin[1])
    gv_ref[...] = jnp.where(low, fin[1], fin[0])
    for half in range(2):
        share(half).wait()
    gq_ref[:, 0:256] = jnp.where(low, qfin[0], qfin[1])
    gq_ref[:, 256:512] = jnp.where(low, qfin[1], qfin[0])


def hand_on(a_ref, b_ref, c_ref, ao_ref, bo_ref, co_ref):
    ao_ref[...] = a_ref[...]
    bo_ref[...] = b_ref[...]
    co_ref[...] = c_ref[...]


VM = pl.BlockSpec(memory_space=pltpu.VMEM)
DMA = pltpu.SemaphoreType.DMA


def per_device(queries, keys, values, output, grad_out, lse, positions):
    partial = pl.pallas_call(
        fused_kernel,
        out_shape=(
            jax.ShapeDtypeStruct((128, 512), BF),
            jax.ShapeDtypeStruct((128, 128), BF),
            jax.ShapeDtypeStruct((128, 128), BF),
        ),
        in_specs=[pl.BlockSpec(memory_space=pltpu.HBM)] * 7,
        out_specs=(VM,) * 3,
        scratch_shapes=[
            pltpu.VMEM((2, 2, 8, 128, 128), BF),
            pltpu.VMEM((8, 8, 128), F32),
            pltpu.VMEM((2, 4, 4, 128, 128), BF),
            pltpu.VMEM((4, 4, 1, 128), jnp.int32),
            pltpu.VMEM((8, 1024), F32),
            pltpu.VMEM((2, 128, 1024), F32),
            pltpu.VMEM((4, 2, 4, 128, 128), F32),
            pltpu.VMEM((4, 4, 128, 128), BF),
            pltpu.VMEM((4, 4, 128, 128), BF),
            pltpu.VMEM((4, 4, 128, 128), BF),
            pltpu.VMEM((2, 64, 128), BF),
            pltpu.VMEM((2, 64, 128), BF),
            pltpu.VMEM((4, 128, 128), BF),
            pltpu.VMEM((4, 128, 128), BF),
            pltpu.VMEM((2, 128, 128), BF),
            pltpu.VMEM((4, 128, 128), BF),
            pltpu.VMEM((4, 128, 128), BF),
            pltpu.VMEM((128, 128), F32),
            pltpu.VMEM((8, 128, 256), BF),
            pltpu.VMEM((8, 128, 256), BF),
            pltpu.VMEM((128, 256), BF),
            pltpu.VMEM((128, 256), BF),
            pltpu.VMEM((2, 128, 128), BF),
            pltpu.VMEM((2, 128, 256), BF),
            pltpu.VMEM((2, 128, 128), BF),
            pltpu.VMEM((4, 128), F32),
            pltpu.VMEM((1, 128), jnp.int32),
            DMA((29,)), DMA((4,)), DMA((4, 4)), DMA((4,)), DMA((2, 6)), DMA((16,)), DMA((4,)), DMA((4, 4)), DMA((7,)),
        ],
        compiler_params=pltpu.CompilerParams(
            collective_id=0, has_side_effects=True, vmem_limit_bytes=24 * 2**20
        ),
        name="attention_grad",
    )(
        *(
            pltpu.with_memory_space_constraint(a, pltpu.HBM)
            for a in (queries, keys, values, output, grad_out, lse, positions.reshape(1, 128))
        )
    )
    return pl.pallas_call(
        hand_on,
        out_shape=tuple(jax.ShapeDtypeStruct(a.shape, a.dtype) for a in partial),
        in_specs=[VM] * 3,
        out_specs=(VM,) * 3,
        compiler_params=pltpu.CompilerParams(vmem_limit_bytes=4 * 2**20),
        name="hand_on",
    )(*partial)


def solution(mesh):
    placed = (
        P("blk", None),
        P("blk", None),
        P("blk", None),
        P("blk", None),
        P("blk", None),
        P(None, "blk"),
        P("blk"),
    )
    return jax.shard_map(
        per_device,
        mesh=mesh,
        in_specs=placed,
        out_specs=(P("blk", None), P("blk", None), P("blk", None)),
        check_vma=False,
    )
```
